512 devices in a mesh: fsdp: 32 (over x, z_lo), member: 16 (over y, z_hi, core).
Axes of the slice: x: 4, y: 4, z: 16 (z_hi: 2, z_lo: 8; z = z_hi * 8 + z_lo), core: 2. Of those that a mesh axis runs over, the one named last changes fastest.
Arguments:
- frames: bfloat16 [16, 4608, 1536], P('member', 'fsdp'), may hold values from -6 to 6
- layer_norm_gain: float32 [1536], replicated, may hold values from 0.25 to 1.75
- input_projection: bfloat16 [1536, 6144], P('fsdp', 'member'), may hold values from -0.15625 to 0.15625
- output_projection: bfloat16 [6144, 1536], P('member', 'fsdp'), may hold values from -0.078125 to 0.078125
- adapter_down_map: bfloat16 [16, 1536, 64], P('member'), may hold values from -0.15625 to 0.15625
- adapter_up_map: bfloat16 [16, 64, 6144], P('member'), may hold values from -0.75 to 0.75
- lengths: int32 [16, 32], P('member', 'fsdp'), may hold values from 90 to 126, as said below
- cotangent: bfloat16 [16, 4608, 1536], P('member', 'fsdp'), may hold values from -0.29882812 to 0.29882812
Outputs:
- down_map_gradient: float32 [16, 1536, 64], P('member')
- up_map_gradient: float32 [16, 64, 6144], P('member')
The draws below stay inside these ranges and needn't reach their ends.
Inputs may be any that keep to these rules, and one draw needn't show every extreme that they name: `lengths`: each member has at least one utterance of exactly 126 frames.
All inputs are finite; a program needn't handle non-finite values.
Results may differ from the reference program's by a relative error of at most 0.0058.
Values may be sent and summed in bfloat16 or wider, within the bound.
A program may use at most 128 MiB of HBM per device.

```python
import jax
import jax.numpy as jnp
from jax import lax

MODEL_WIDTH = 1536
HIDDEN_UNITS = 6144
ADAPTER_RANK = 64
BUCKET = 144
LMAX = 126
ADJUST_MEMBERS = 16
UTTS = 32
FRAMES = 4608


def draw_lengths(key, part):
    key_len = jax.random.fold_in(key, 11)
    key_pick = jax.random.fold_in(key, 12)
    values = jax.random.randint(key_len, (ADJUST_MEMBERS, UTTS), 5 * BUCKET // 8, LMAX + 1, dtype=jnp.int32)
    chosen = jax.random.randint(key_pick, (ADJUST_MEMBERS,), 0, UTTS, dtype=jnp.int32)
    slots = jnp.arange(UTTS, dtype=jnp.int32)[None, :]
    return jnp.where(slots == chosen[:, None], jnp.int32(LMAX), values)


def shard_levels(key, shape, shards, least, top_value):
    def one(position, shards_of):
        heights = jax.random.uniform(jax.random.fold_in(jax.random.fold_in(key, 6), position), (shards_of,), jnp.float32, least / len(shards), top_value / len(shards))
        return jnp.repeat(jnp.exp(heights), shape[position] // shards_of).reshape((-1,) + (1,) * (len(shape) - position - 1))

    loudness = one(*shards[0])
    for cut in shards[1:]:
        loudness = loudness * one(*cut)
    return loudness


def gaussian(rng, shape, scale, limit, cuts=(), kind=jnp.bfloat16):
    values = jax.random.normal(rng, shape, jnp.float32) * scale
    if len(cuts) > 0:
        values = shard_levels(rng, shape, cuts, -0.22, 0.18) * values
    return jnp.clip(values, min=-limit, max=limit).astype(kind)


def setup_inputs(seed: int = 0) -> dict:
    seeds = jax.random.split(jax.random.key(seed), 9)
    return {
        "frames": gaussian(seeds[0], (ADJUST_MEMBERS, FRAMES, MODEL_WIDTH), 1.0, 6.0, ((0, 16), (1, 32))),
        "layer_norm_gain": jnp.clip(1.0 + 0.15 * jax.random.normal(seeds[1], (MODEL_WIDTH,), jnp.float32), 0.25, 1.75),
        "input_projection": gaussian(seeds[2], (MODEL_WIDTH, HIDDEN_UNITS), MODEL_WIDTH ** -0.5, 0.15625, ((0, 32), (1, 16))),
        "output_projection": gaussian(seeds[3], (HIDDEN_UNITS, MODEL_WIDTH), HIDDEN_UNITS ** -0.5, 0.078125, ((0, 16), (1, 32))),
        "adapter_down_map": gaussian(seeds[4], (ADJUST_MEMBERS, MODEL_WIDTH, ADAPTER_RANK), MODEL_WIDTH ** -0.5, 0.15625, ((0, 16),)),
        "adapter_up_map": gaussian(seeds[5], (ADJUST_MEMBERS, ADAPTER_RANK, HIDDEN_UNITS), ADAPTER_RANK ** -0.5, 0.75, ((0, 16),)),
        "lengths": draw_lengths(jax.random.fold_in(seeds[8], 71), 0),
        "cotangent": gaussian(seeds[7], (ADJUST_MEMBERS, FRAMES, MODEL_WIDTH), 0.05, 0.29882812, ((0, 16), (1, 32))),
    }


def reference(frames, layer_norm_gain, input_projection, output_projection, adapter_down_map, adapter_up_map, lengths, cotangent):
    positions = jnp.arange(BUCKET, dtype=jnp.int32)

    def member_gradient_list(packed):
        block, down, up, sizes, cot = packed
        values = block.astype(jnp.float32)
        mean = lax.optimization_barrier(jnp.mean(values, axis=1, keepdims=True))
        var = lax.optimization_barrier(jnp.mean((values - mean) ** 2, axis=1, keepdims=True))
        normed_input = (layer_norm_gain * (values - mean) / jnp.sqrt(var + 1e-05)).astype(jnp.bfloat16)
        low_rank_state = jnp.dot(normed_input, down, preferred_element_type=jnp.float32).astype(jnp.bfloat16)
        pre = jnp.dot(normed_input, input_projection, preferred_element_type=jnp.float32) + jnp.dot(low_rank_state, up, preferred_element_type=jnp.float32)
        mask = (positions[None, :] < sizes[:, None]).reshape(-1)
        masked = cot * mask.astype(cot.dtype)[:, None]
        dhid = 0.5 * jnp.dot(masked, output_projection.T, preferred_element_type=jnp.float32)
        sig = jax.nn.sigmoid(pre)
        dpre = (dhid * sig * (1.0 + pre * (1.0 - sig))).astype(jnp.bfloat16)
        up_map_gradient = jnp.dot(low_rank_state.T, dpre, preferred_element_type=jnp.float32)
        back = jnp.dot(dpre, up.T, preferred_element_type=jnp.float32).astype(jnp.bfloat16)
        down_map_gradient = jnp.dot(normed_input.T, back, preferred_element_type=jnp.float32)
        return (down_map_gradient, up_map_gradient)
    down_map_gradient, up_map_gradient = lax.map(member_gradient_list, (frames, adapter_down_map, adapter_up_map, lengths, cotangent))
    return (down_map_gradient, up_map_gradient)
```

```python
import jax
import jax.numpy as jnp
from jax import lax
from jax.experimental import pallas as pl
from jax.experimental.pallas import tpu as pltpu
from jax.sharding import PartitionSpec as P

MESH = pl.DeviceIdType.MESH
ROWS = 128
D = 1536
RANK = 64
LOW = D
COT = D + 128
WIDE = 2 * D + 128
F32 = jnp.float32
BF16 = jnp.bfloat16


def dot(a, b, dims=((1,), (0,))):
    return lax.dot_general(a, b, (dims, ((), ())), preferred_element_type=F32)


def kernel(
    frames, gain, w1, w2, down_map, up_map, lengths, cot,
    dn_out, up_out,
    ws_a, ws_b, wa, wb, tok, ub, bks, bkr, bka, rss, rsr, dns, dnr, ag,
    tp_s, tp_r, tk_s, tk_r, td_s, td_r, u_s, u_r,
    ay_s, ay_r, az_s, az_r, bz_s, bz_r, by_s, by_r, bo_s, bo_r,
    bk_s, bk_r, ba_s, ba_r, rs_s, rs_r, dn_s, dn_r, gz_s, gz_r, gx_s, gx_r,
):
    fi = lax.axis_index("fsdp")
    mi = lax.axis_index("member")
    x, zl = fi // 8, fi % 8
    y, zh, c = mi // 4, (mi // 2) % 2, mi % 2
    z = zh * 8 + zl

    def dev(x_, y_, z_, c_):
        return (x_ * 8 + z_ % 8, y_ * 4 + (z_ // 8) * 2 + c_)

    xr, xl, xo = (x + 1) % 4, (x + 3) % 4, (x + 2) % 4
    yr, yl, yo = (y + 1) % 4, (y + 3) % 4, (y + 2) % 4
    right, left = dev(xr, y, z, c), dev(xl, y, z, c)
    up, dn = dev(x, yr, z, c), dev(x, yl, z, c)
    fore, aft = dev(x, y, (z + 1) % 16, c), dev(x, y, (z + 15) % 16, c)
    twin = dev(x, y, z, 1 - c)
    flip = dev(y, x, z, c)

    def zdev(d, c_):
        return dev(x, y, zh * 8 + (zl + d) % 8, c_)

    def rcopy(src, dst, ss, rs, to):
        return pltpu.make_async_remote_copy(
            src_ref=src, dst_ref=dst, send_sem=ss, recv_sem=rs, device_id=to, device_id_type=MESH
        )

    barrier = pltpu.get_barrier_semaphore()
    peers = [up, dn, fore, aft, twin]
    for d in range(1, 4):
        for c_ in range(2):
            peers.append(dev((x + d) % 4, y, z, c_))
    for d in range(1, 8):
        for c_ in range(2):
            peers.append(zdev(d, c_))
    for peer in peers:
        pl.semaphore_signal(barrier, inc=1, device_id=peer, device_id_type=MESH)

    @pl.when(x != y)
    def _():
        pl.semaphore_signal(barrier, inc=1, device_id=flip, device_id_type=MESH)

    eye = (
        lax.broadcasted_iota(jnp.int32, (48, 48), 0) == lax.broadcasted_iota(jnp.int32, (48, 48), 1)
    ).astype(BF16)
    w2t = dot(eye, w2[...], ((1,), (1,))).astype(BF16)
    ws_a[0] = w1[:, 0:128]
    ws_b[0] = w1[:, 128:384]
    ws_a[1] = w2t[:, 0:128]
    ws_b[1] = w2t[:, 128:384]

    pl.semaphore_wait(barrier, len(peers) + jnp.where(x != y, 1, 0))

    def tp_copies():
        return [
            rcopy(ws_a.at[0], wa.at[zh, x, zl], tp_s.at[0], tp_r.at[0], flip),
            rcopy(ws_a.at[1], wa.at[zh, 4 + x, zl], tp_s.at[1], tp_r.at[1], flip),
            rcopy(ws_b, wb.at[zh, :, x, zl], tp_s.at[2], tp_r.at[2], flip),
        ]

    @pl.when(x != y)
    def _():
        for cp in tp_copies():
            cp.start()

    @pl.when(x == y)
    def _():
        for w in range(2):
            wa[zh, 4 * w + y, zl] = ws_a[w]
            wb[zh, w, y, zl] = ws_b[w]

    v = frames[0, 0:ROWS, :].astype(F32)
    mean = jnp.mean(v, axis=1, keepdims=True)
    var = jnp.mean((v - mean) ** 2, axis=1, keepdims=True)
    normed = (gain[...] * (v - mean) / jnp.sqrt(var + 1e-05)).astype(BF16)
    low = dot(normed, down_map[0]).astype(BF16)
    keep = lax.broadcasted_iota(jnp.int32, (ROWS, D), 0) < lengths[0, 0]
    masked = jnp.where(keep, cot[0, 0:ROWS, :].astype(F32), 0.0).astype(BF16)
    tok[x, c, :, 0:D] = normed
    tok[x, c, :, LOW : LOW + 128] = jnp.concatenate([low, jnp.zeros_like(low)], axis=1)
    tok[x, c, :, COT:WIDE] = masked

    def half(x_, h):
        return tok.at[x_, c, pl.ds(64 * h, 64), :]

    def halfo(x_, h):
        return tok.at[x_, 1 - c, pl.ds(64 * h, 64), :]

    def t_copy(i):
        x_, h, to = [
            (x, 0, right), (x, 1, right), (x, 1, left), (x, 0, left), (xl, 0, right), (xr, 1, left)
        ][i]
        return rcopy(half(x_, h), half(x_, h), tk_s.at[i], tk_r.at[i], to)

    def t_wait(i):
        x_, h = [(xl, 0), (xl, 1), (xr, 1), (xr, 0), (xo, 0), (xo, 1)][i]
        rcopy(half(x_, h), half(x_, h), tk_s.at[i], tk_r.at[i], right).wait_recv()

    def d_copy(r, h):
        x_ = [x, xl, xr, xo][r]
        return rcopy(half(x_, h), half(x_, h), td_s.at[2 * r + h], td_r.at[2 * r + h], twin)

    def d_wait(r, h):
        x_ = [x, xl, xr, xo][r]
        rcopy(halfo(x_, h), halfo(x_, h), td_s.at[2 * r + h], td_r.at[2 * r + h], twin).wait_recv()

    for i in (0, 2, 1, 3):
        t_copy(i).start()

    def a_blk(s):
        z_ = (z + s + 16) % 16
        return wa.at[z_ // 8, :, z_ % 8]

    def a_half(s, w):
        z_ = (z + s + 16) % 16
        return wa.at[z_ // 8, pl.ds(4 * w, 4), z_ % 8]

    def a_one(y_, w):
        return wa.at[zh, 4 * w + y_, zl]

    def b_blk(s, y_):
        z_ = (z + s + 16) % 16
        return wb.at[z_ // 8, :, y_, z_ % 8]

    def b_half(s, y_, w):
        z_ = (z + s + 16) % 16
        return wb.at[z_ // 8, w, y_, z_ % 8]

    def ay_copy(i):
        y_, w, to = [(y, 0, up), (y, 1, up), (y, 0, dn), (y, 1, dn), (yl, 0, up), (yr, 1, dn)][i]
        return rcopy(a_one(y_, w), a_one(y_, w), ay_s.at[i], ay_r.at[i], to)

    def ay_wait(i):
        y_, w = [(yl, 0), (yl, 1), (yr, 0), (yr, 1), (yo, 0), (yo, 1)][i]
        rcopy(a_one(y_, w), a_one(y_, w), ay_s.at[i], ay_r.at[i], up).wait_recv()

    def z_full(route, k, make, ss, rs):
        s = (-(k - 1)) if route == 0 else (k - 1)
        return rcopy(make(s), make(s), ss.at[route, k], rs.at[route, k], fore if route == 0 else aft)

    def z_half(route, make, ss, rs):
        s = -7 if route == 0 else 7
        return rcopy(make(s, route), make(s, route), ss.at[route, 8], rs.at[route, 8], fore if route == 0 else aft)

    def z_wait(route, k, make, ss, rs):
        s = -k if route == 0 else k
        rcopy(make(s), make(s), ss.at[route, k], rs.at[route, k], fore).wait_recv()

    def z_wait_half(route, make, ss, rs):
        rcopy(make(8, route), make(8, route), ss.at[route, 8], rs.at[route, 8], fore).wait_recv()

    def b_own(s):
        return b_blk(s, y)

    def b_own_half(s, w):
        return b_half(s, y, w)

    def by_copy(s, j, way):
        return rcopy(b_blk(s, y), b_blk(s, y), by_s.at[way, j], by_r.at[way, j], up if way == 0 else dn)

    def by_wait(s, j, way):
        y_ = yl if way == 0 else yr
        rcopy(b_blk(s, y_), b_blk(s, y_), by_s.at[way, j], by_r.at[way, j], up).wait_recv()

    def bo_copy(s, j, way):
        y_ = yl if way == 0 else yr
        return rcopy(
            b_half(s, y_, way), b_half(s, y_, way), bo_s.at[way, j], bo_r.at[way, j], up if way == 0 else dn
        )

    def bo_wait(s, j, way):
        rcopy(b_half(s, yo, way), b_half(s, yo, way), bo_s.at[way, j], bo_r.at[way, j], up).wait_recv()

    @pl.when(x != y)
    def _():
        for cp in tp_copies():
            cp.wait_recv()

    for i in range(4):
        ay_copy(i).start()
    for route in range(2):
        z_full(route, 1, b_own, bz_s, bz_r).start()
    for way in range(2):
        by_copy(0, 0, way).start()

    for h in range(2):
        d_copy(0, h).start()

    def u_cols(zh_, c_):
        return up_map.at[0, :, pl.ds(pl.multiple_of(((x * 2 + zh_) * 2 + c_) * 384, 128), 384)]

    def u_local(zh_):
        return pltpu.make_async_copy(u_cols(zh_, c), ub.at[c, zh_], u_s.at[2 + zh_])

    def u_copy(zh_):
        return rcopy(u_cols(zh_, 1 - c), ub.at[c, zh_], u_s.at[zh_], u_r.at[zh_], twin)

    for zh_ in range(2):
        u_local(zh_).start()
        u_copy(zh_).start()

    ay_wait(0)
    ay_copy(4).start()
    ay_wait(3)
    ay_copy(5).start()
    for i in (1, 2, 4, 5):
        ay_wait(i)
    for route in range(2):
        z_full(route, 1, a_blk, az_s, az_r).start()

    def y_stage(s, j):
        for way in range(2):
            by_wait(s, j, way)
            bo_copy(s, j, way).start()

    def step(k, _):
        for route in range(2):
            z_wait(route, k, b_own, bz_s, bz_r)
            z_full(route, k + 1, b_own, bz_s, bz_r).start()
            s = -k if route == 0 else k
            for way in range(2):
                by_copy(s, 2 * k - 1 + route, way).start()
        for route in range(2):
            z_wait(route, k, a_blk, az_s, az_r)
            z_full(route, k + 1, a_blk, az_s, az_r).start()
        for route in range(2):
            s = -(k - 1) if route == 0 else (k - 1)

            @pl.when((k > 1) | (route == 0))
            def _():
                y_stage(s, jnp.where(k == 1, 0, 2 * k - 3 + route))
        return 0

    lax.fori_loop(1, 4, step, 0)
    t_wait(0)
    t_copy(4).start()
    d_copy(1, 0).start()
    t_wait(2)
    t_copy(5).start()
    d_copy(2, 1).start()
    lax.fori_loop(4, 7, step, 0)
    t_wait(1)
    d_copy(1, 1).start()
    t_wait(3)
    d_copy(2, 0).start()
    for route in range(2):
        z_wait(route, 7, b_own, bz_s, bz_r)
        z_half(route, b_own_half, bz_s, bz_r).start()
        s = -7 if route == 0 else 7
        for way in range(2):
            by_copy(s, 13 + route, way).start()
    for route in range(2):
        z_wait(route, 7, a_blk, az_s, az_r)
        z_half(route, a_half, az_s, az_r).start()
    y_stage(-6, 11)
    y_stage(6, 12)
    for route in range(2):
        z_wait_half(route, b_own_half, bz_s, bz_r)
    for way in range(2):
        by_copy(8, 15, way).start()
    for route in range(2):
        z_wait_half(route, a_half, az_s, az_r)
    y_stage(-7, 13)
    y_stage(7, 14)
    for i in (4, 5):
        t_wait(i)
        d_copy(3, i - 4).start()
    y_stage(8, 15)

    def bo_step(j, _):
        s = jnp.where(j % 2 == 1, -((j + 1) // 2), (j + 1) // 2)
        for way in range(2):
            bo_wait(s, j, way)
        return 0

    for way in range(2):
        bo_wait(0, 0, way)
    lax.fori_loop(1, 15, bo_step, 0)
    for way in range(2):
        bo_wait(8, 15, way)
    for r in range(4):
        for h in range(2):
            d_wait(r, h)
    for zh_ in range(2):
        u_local(zh_).wait()
        rcopy(ub.at[1 - c, zh_], ub.at[1 - c, zh_], u_s.at[zh_], u_r.at[zh_], twin).wait_recv()

    def member(m, _):
        lo = tok[:, m, :, LOW : LOW + 128].reshape(4 * ROWS, 128)
        for b in range(4):
            zh_, is_b = b // 2, b % 2
            c0, c1 = (128, 384) if is_b else (0, 128)
            if is_b:
                wi, wo = wb[zh_, 0].reshape(D, 256), wb[zh_, 1].reshape(D, 256)
            else:
                wi, wo = wa[zh_, 0:4].reshape(D, 128), wa[zh_, 4:8].reshape(D, 128)
            u = ub[m, zh_, :, c0:c1]
            pre = dot(tok[:, m, :, 0:D].reshape(4 * ROWS, D), wi) + dot(lo[:, 0:RANK], u)
            dhid = 0.5 * dot(tok[:, m, :, COT:WIDE].reshape(4 * ROWS, D), wo)
            sig = jax.nn.sigmoid(pre)
            dpre = (dhid * sig * (1.0 + pre * (1.0 - sig))).astype(BF16)
            part = dot(lo, dpre, ((0,), (0,)))
            for r in range(8):
                rss[m, r, :, zh_ * 384 + c0 : zh_ * 384 + c1] = part[8 * r : 8 * r + 8].astype(BF16)
            for x_ in range(4):
                bp = dot(u, dpre[ROWS * x_ : ROWS * (x_ + 1)], ((1,), (1,)))
                if b == 0:
                    bks[x_, m] = bp
                else:
                    bks[x_, m] += bp
        return 0

    lax.fori_loop(0, 2, member, 0)

    def bk_copy(d, c_):
        x_ = (x + d) % 4
        return rcopy(bks.at[x_, c_], bkr.at[x, c], bk_s.at[d, c_], bk_r.at[d, c], dev(x_, y, z, c_))

    def bk_other():
        return rcopy(bks.at[x, 1 - c], bkr.at[x, c], bk_s.at[0, 0], bk_r.at[0, 0], twin)

    bk_other().start()
    for d in range(1, 4):
        for c_ in range(2):
            bk_copy(d, c_).start()

    def rs_copy(d, c_):
        return rcopy(rss.at[c_, (zl + d) % 8], rsr.at[zl, c], rs_s.at[d, c_], rs_r.at[d, c], zdev(d, c_))

    def rs_other():
        return rcopy(rss.at[1 - c, zl], rsr.at[zl, c], rs_s.at[0, 0], rs_r.at[0, 0], twin)

    rs_other().start()
    for d in range(1, 8):
        for c_ in range(2):
            rs_copy(d, c_).start()
    rsr[zl, c] = rss[c, zl]
    bkr[x, c] = bks[x, c]

    rcopy(bkr.at[x, 1 - c], bkr.at[x, 1 - c], bk_s.at[0, 0], bk_r.at[0, 0], twin).wait_recv()
    for d in range(1, 4):
        for c_ in range(2):
            slot = bkr.at[(x + 4 - d) % 4, c_]
            rcopy(slot, slot, bk_s.at[d, c_], bk_r.at[d, c_], twin).wait_recv()
    total = bkr[0, 0]
    for i in range(1, 8):
        total = total + bkr[i // 2, i % 2]
    bka[x] = total.astype(BF16)

    def ba_copy(d):
        return rcopy(bka.at[x], bka.at[x], ba_s.at[d], ba_r.at[d], dev((x + d) % 4, y, z, c))

    for d in range(1, 4):
        ba_copy(d).start()
    for d in range(1, 4):
        slot = bka.at[(x + 4 - d) % 4]
        rcopy(slot, slot, ba_s.at[d], ba_r.at[d], right).wait_recv()
    quarter = pl.ds(pl.multiple_of(x * 384, 128), 384)
    part = dot(bka[0], tok[0, c, :, quarter])
    for x_ in range(1, 4):
        part = part + dot(bka[x_], tok[x_, c, :, quarter])
    for r in range(8):
        dns[r] = part[8 * r : 8 * r + 8].astype(BF16)

    def dn_copy(d):
        return rcopy(dns.at[(zl + d) % 8], dnr.at[zl], dn_s.at[d], dn_r.at[d], zdev(d, c))

    for d in range(1, 8):
        dn_copy(d).start()
    dnr[zl] = dns[zl]

    other = rsr.at[zl, 1 - c]
    rcopy(other, other, rs_s.at[0, 0], rs_r.at[0, 0], twin).wait_recv()
    for d in range(1, 8):
        for c_ in range(2):
            slot = rsr.at[(zl + 8 - d) % 8, c_]
            rcopy(slot, slot, rs_s.at[d, c_], rs_r.at[d, c_], twin).wait_recv()
    for c_ in range(2):
        total = rsr[0, c_].astype(F32)
        for i in range(1, 8):
            total = total + rsr[i, c_].astype(F32)
        ag[x, zl, :, 768 * c_ : 768 * (c_ + 1)] = total.astype(BF16)
    for d in range(1, 8):
        slot = dnr.at[(zl + 8 - d) % 8]
        rcopy(slot, slot, dn_s.at[d], dn_r.at[d], twin).wait_recv()
    total = dnr[0].astype(F32)
    for i in range(1, 8):
        total = total + dnr[i].astype(F32)
    ag[x, zl, :, 1536:1920] = total.astype(BF16)

    def gz_copy(d):
        return rcopy(ag.at[x, zl], ag.at[x, zl], gz_s.at[d], gz_r.at[d], zdev(d, c))

    for d in range(1, 8):
        gz_copy(d).start()
    for d in range(1, 8):
        slot = ag.at[x, (zl + 8 - d) % 8]
        rcopy(slot, slot, gz_s.at[d], gz_r.at[d], right).wait_recv()

    def g_half(x_, h):
        return ag.at[x_, pl.ds(4 * h, 4)]

    def gx_copy(i):
        x_, h, to = [
            (x, 0, right), (x, 1, right), (x, 1, left), (x, 0, left), (xl, 0, right), (xr, 1, left)
        ][i]
        return rcopy(g_half(x_, h), g_half(x_, h), gx_s.at[i], gx_r.at[i], to)

    def gx_wait(i):
        x_, h = [(xl, 0), (xl, 1), (xr, 1), (xr, 0), (xo, 0), (xo, 1)][i]
        rcopy(g_half(x_, h), g_half(x_, h), gx_s.at[i], gx_r.at[i], right).wait_recv()

    for i in (0, 2, 1, 3):
        gx_copy(i).start()
    gx_wait(0)
    gx_copy(4).start()
    gx_wait(2)
    gx_copy(5).start()
    for i in (1, 3, 4, 5):
        gx_wait(i)

    def write(i, _):
        rows = pl.ds(pl.multiple_of(8 * i, 8), 8)
        for x_ in range(4):
            for c_ in range(2):
                for h in range(2):
                    col = ((x_ * 2 + h) * 2 + c_) * 384
                    src = 768 * c_ + 384 * h
                    up_out[rows, col : col + 384] = ag[x_, i, :, src : src + 384].astype(F32)
            dn_out[rows, 384 * x_ : 384 * (x_ + 1)] = ag[x_, i, :, 1536:1920].astype(F32)
        return 0

    lax.fori_loop(0, 8, write, 0)

    @pl.when(x != y)
    def _():
        for cp in tp_copies():
            cp.wait_send()

    for i in range(6):
        t_copy(i).wait_send()
        ay_copy(i).wait_send()
        gx_copy(i).wait_send()
    for r in range(4):
        for h in range(2):
            d_copy(r, h).wait_send()
    for zh_ in range(2):
        u_copy(zh_).wait_send()
    for route in range(2):
        def z_sent(k, _):
            z_full(route, k, b_own, bz_s, bz_r).wait_send()
            z_full(route, k, a_blk, az_s, az_r).wait_send()
            return 0

        lax.fori_loop(1, 8, z_sent, 0)
        z_half(route, b_own_half, bz_s, bz_r).wait_send()
        z_half(route, a_half, az_s, az_r).wait_send()

        def y_sent(j, _):
            by_copy(0, j, route).wait_send()
            bo_copy(0, j, route).wait_send()
            return 0

        lax.fori_loop(0, 16, y_sent, 0)
    bk_other().wait_send()
    rs_other().wait_send()
    for c_ in range(2):
        for d in range(1, 4):
            bk_copy(d, c_).wait_send()
        for d in range(1, 8):
            rs_copy(d, c_).wait_send()
    for d in range(1, 4):
        ba_copy(d).wait_send()
    for d in range(1, 8):
        dn_copy(d).wait_send()
        gz_copy(d).wait_send()


def on_device(frames, gain, w1, w2, down_map, up_map, lengths, cot):
    vmem = pl.BlockSpec(memory_space=pltpu.VMEM)
    dma = pltpu.SemaphoreType.DMA
    dn, up = pl.pallas_call(
        kernel,
        out_shape=(
            jax.ShapeDtypeStruct((RANK, D), F32),
            jax.ShapeDtypeStruct((RANK, 6144), F32),
        ),
        in_specs=[vmem, vmem, vmem, vmem, vmem, pl.BlockSpec(memory_space=pl.ANY),
                  pl.BlockSpec(memory_space=pltpu.SMEM), vmem],
        out_specs=(vmem, vmem),
        scratch_shapes=[
            pltpu.VMEM((2, 48, 128), BF16),
            pltpu.VMEM((2, 48, 256), BF16),
            pltpu.VMEM((2, 8, 8, 48, 128), BF16),
            pltpu.VMEM((2, 2, 4, 8, 48, 256), BF16),
            pltpu.VMEM((4, 2, ROWS, WIDE), BF16),
            pltpu.VMEM((2, 2, RANK, 384), BF16),
            pltpu.VMEM((4, 2, RANK, ROWS), F32),
            pltpu.VMEM((4, 2, RANK, ROWS), F32),
            pltpu.VMEM((4, RANK, ROWS), BF16),
            pltpu.VMEM((2, 8, 8, 768), BF16),
            pltpu.VMEM((8, 2, 8, 768), BF16),
            pltpu.VMEM((8, 8, 384), BF16),
            pltpu.VMEM((8, 8, 384), BF16),
            pltpu.VMEM((4, 8, 8, 1920), BF16),
            dma((3,)), dma((3,)), dma((6,)), dma((6,)), dma((8,)), dma((8,)), dma((4,)), dma((2,)),
            dma((6,)), dma((6,)), dma((2, 9)), dma((2, 9)), dma((2, 9)), dma((2, 9)),
            dma((2, 16)), dma((2, 16)), dma((2, 16)), dma((2, 16)),
            dma((4, 2)), dma((4, 2)), dma((4,)), dma((4,)), dma((8, 2)), dma((8, 2)),
            dma((8,)), dma((8,)), dma((8,)), dma((8,)), dma((6,)), dma((6,)),
        ],
        compiler_params=pltpu.CompilerParams(
            collective_id=0, has_side_effects=True, vmem_limit_bytes=56 * 1024 * 1024
        ),
    )(frames, gain.reshape(1, D), w1, w2, down_map, up_map, lengths, cot)
    return dn.T[None], up[None]


def solution(mesh):
    in_specs = (
        P("member", "fsdp", None),
        P(),
        P("fsdp", "member"),
        P("member", "fsdp"),
        P("member", None, None),
        P("member", None, None),
        P("member", "fsdp"),
        P("member", "fsdp", None),
    )
    out_specs = (P("member", None, None), P("member", None, None))
    return jax.shard_map(
        on_device, mesh=mesh, in_specs=in_specs, out_specs=out_specs, check_vma=False
    )
```

```python
import jax
import jax.numpy as jnp
from jax import lax
from jax.experimental import pallas as pl
from jax.experimental.pallas import tpu as pltpu
from jax.sharding import PartitionSpec as P

MESH = pl.DeviceIdType.MESH
ROWS = 128
D = 1536
RANK = 64
LOW = D
COT = D + 128
WIDE = 2 * D + 128
F32 = jnp.float32
BF16 = jnp.bfloat16


def dot(a, b, dims=((1,), (0,))):
    return lax.dot_general(a, b, (dims, ((), ())), preferred_element_type=F32)


def kernel(
    frames, gain, w1, w2t, down_map, up_map, lengths, cot,
    ag,
    ws_a, ws_b, wa, wb, tok, ub, bks, bkr, bka, rss, rsr, dns, dnr,
    ta_s, ta_r, tb_s, tb_r, tk_s, tk_r, td_s, td_r, u_s, u_r,
    az_s, az_r, bz_s, bz_r, by_s, by_r, bo_s, bo_r,
    bk_s, bk_r, ba_s, ba_r, rs_s, rs_r, dn_s, dn_r, gz_s, gz_r, gx_s, gx_r,
):
    fi = lax.axis_index("fsdp")
    mi = lax.axis_index("member")
    x, zl = fi // 8, fi % 8
    y, zh, c = mi // 4, (mi // 2) % 2, mi % 2
    z = zh * 8 + zl

    def dev(x_, y_, z_, c_):
        return (x_ * 8 + z_ % 8, y_ * 4 + (z_ // 8) * 2 + c_)

    xr, xl, xo = (x + 1) % 4, (x + 3) % 4, (x + 2) % 4
    yr, yl, yo = (y + 1) % 4, (y + 3) % 4, (y + 2) % 4
    right, left = dev(xr, y, z, c), dev(xl, y, z, c)
    up, dn = dev(x, yr, z, c), dev(x, yl, z, c)
    fore, aft = dev(x, y, (z + 1) % 16, c), dev(x, y, (z + 15) % 16, c)
    twin = dev(x, y, z, 1 - c)
    flip = dev(y, x, z, c)

    def zdev(d, c_):
        return dev(x, y, zh * 8 + (zl + d) % 8, c_)

    def rcopy(src, dst, ss, rs, to):
        return pltpu.make_async_remote_copy(
            src_ref=src, dst_ref=dst, send_sem=ss, recv_sem=rs, device_id=to, device_id_type=MESH
        )

    barrier = pltpu.get_barrier_semaphore()
    peers = [up, dn, dev(x, yo, z, c), fore, aft, twin]
    for d in range(1, 4):
        for c_ in range(2):
            peers.append(dev((x + d) % 4, y, z, c_))
    for d in range(1, 8):
        for c_ in range(2):
            peers.append(zdev(d, c_))
    for peer in peers:
        pl.semaphore_signal(barrier, inc=1, device_id=peer, device_id_type=MESH)

    for e in range(1, 4):
        for peer in (dev((x + e) % 4, x, z, c),):
            pl.semaphore_signal(barrier, inc=1, device_id=peer, device_id_type=MESH)

    @pl.when(x != y)
    def _():
        pl.semaphore_signal(barrier, inc=1, device_id=dev(x, x, z, c), device_id_type=MESH)
        pl.semaphore_signal(barrier, inc=1, device_id=flip, device_id_type=MESH)

    ws_a[0] = w1[:, 0:128]
    ws_b[0] = w1[:, 128:384]
    ws_a[1] = w2t[:, 0:128]
    ws_b[1] = w2t[:, 128:384]

    pl.semaphore_wait(barrier, len(peers) + jnp.where(x != y, 5, 3))

    def ta_copy(e):
        to = dev(y, (y + e) % 4, z, c)
        return rcopy(ws_a, wa.at[zh, :, x, zl], ta_s.at[e], ta_r.at[x], to)

    def ta_wait(a):
        slot = wa.at[zh, :, a, zl]
        rcopy(slot, slot, ta_s.at[0], ta_r.at[a], flip).wait_recv()

    def tb_copy():
        return rcopy(ws_b, wb.at[zh, :, x, zl], tb_s.at[0], tb_r.at[0], flip)

    @pl.when(x != y)
    def _():
        tb_copy().start()
        ta_copy(0).start()

    @pl.when(x == y)
    def _():
        for w in range(2):
            wa[zh, w, y, zl] = ws_a[w]
            wb[zh, w, y, zl] = ws_b[w]

    for e in range(1, 4):
        ta_copy(e).start()

    v = frames[0, 0:ROWS, :].astype(F32)
    mean = jnp.mean(v, axis=1, keepdims=True)
    var = jnp.mean((v - mean) ** 2, axis=1, keepdims=True)
    normed = (gain[...][None, :] * (v - mean) / jnp.sqrt(var + 1e-05)).astype(BF16)
    low = dot(normed, down_map[...], ((1,), (1,))).astype(BF16)
    keep = lax.broadcasted_iota(jnp.int32, (ROWS, D), 0) < lengths[0, 0]
    masked = jnp.where(keep, cot[0, 0:ROWS, :].astype(F32), 0.0).astype(BF16)
    tok[x, c, :, 0:D] = normed
    tok[x, c, :, LOW : LOW + 128] = jnp.concatenate([low, jnp.zeros_like(low)], axis=1)
    tok[x, c, :, COT:WIDE] = masked

    def half(x_, h):
        return tok.at[x_, c, pl.ds(64 * h, 64), :]

    def halfo(x_, h):
        return tok.at[x_, 1 - c, pl.ds(64 * h, 64), :]

    def t_copy(i):
        x_, h, to = [
            (x, 0, right), (x, 1, right), (x, 1, left), (x, 0, left), (xl, 0, right), (xr, 1, left)
        ][i]
        return rcopy(half(x_, h), half(x_, h), tk_s.at[i], tk_r.at[i], to)

    def t_wait(i):
        x_, h = [(xl, 0), (xl, 1), (xr, 1), (xr, 0), (xo, 0), (xo, 1)][i]
        rcopy(half(x_, h), half(x_, h), tk_s.at[i], tk_r.at[i], right).wait_recv()

    def d_copy(r, h):
        x_ = [x, xl, xr, xo][r]
        return rcopy(half(x_, h), half(x_, h), td_s.at[2 * r + h], td_r.at[2 * r + h], twin)

    def d_wait(r, h):
        x_ = [x, xl, xr, xo][r]
        rcopy(halfo(x_, h), halfo(x_, h), td_s.at[2 * r + h], td_r.at[2 * r + h], twin).wait_recv()

    for i in (0, 2, 1, 3):
        t_copy(i).start()

    def a_str(s, w):
        z_ = (z + s + 16) % 16
        return wa.at[z_ // 8, w, :, z_ % 8]

    def b_str(s, w):
        return b_half(s, y, w)

    def b_blk(s, y_):
        z_ = (z + s + 16) % 16
        return wb.at[z_ // 8, :, y_, z_ % 8]

    def b_half(s, y_, w):
        z_ = (z + s + 16) % 16
        return wb.at[z_ // 8, w, y_, z_ % 8]

    streams = [(b_str, bz_s, bz_r), (a_str, az_s, az_r)]

    def z_copy(i, w, route, k):
        make, ss, rs = streams[i]
        blk = make((-(k - 1)) if route == 0 else (k - 1), w)
        return rcopy(blk, blk, ss.at[route, w, k], rs.at[route, w, k], fore if route == 0 else aft)

    def z_wait(i, w, route, k):
        make, ss, rs = streams[i]
        blk = make(-k if route == 0 else k, w)
        rcopy(blk, blk, ss.at[route, w, k], rs.at[route, w, k], fore).wait_recv()

    def by_copy(s, j, way):
        return rcopy(b_blk(s, y), b_blk(s, y), by_s.at[way, j], by_r.at[way, j], up if way == 0 else dn)

    def by_wait(s, j, way):
        y_ = yl if way == 0 else yr
        rcopy(b_blk(s, y_), b_blk(s, y_), by_s.at[way, j], by_r.at[way, j], up).wait_recv()

    def by_last(way):
        blk = b_blk(8, y)
        return rcopy(blk, blk, by_s.at[way, 15], by_r.at[way, 15], [up, dn, dev(x, yo, z, c)][way])

    def by_last_wait(way):
        blk = b_blk(8, [yl, yr, yo][way])
        rcopy(blk, blk, by_s.at[way, 15], by_r.at[way, 15], up).wait_recv()

    def bo_copy(s, j, way):
        y_ = yl if way == 0 else yr
        return rcopy(
            b_half(s, y_, way), b_half(s, y_, way), bo_s.at[way, j], bo_r.at[way, j], up if way == 0 else dn
        )

    def bo_wait(s, j, way):
        rcopy(b_half(s, yo, way), b_half(s, yo, way), bo_s.at[way, j], bo_r.at[way, j], up).wait_recv()

    @pl.when(x != y)
    def _():
        blk = wb.at[zh, :, y, zl]
        rcopy(blk, blk, tb_s.at[0], tb_r.at[0], flip).wait_recv()

    for w in range(2):
        for route in range(2):
            z_copy(0, w, route, 1).start()
    for way in range(2):
        by_copy(0, 0, way).start()
    for e in range(1, 4):
        ta_wait((x + e) % 4)

    @pl.when(x != y)
    def _():
        ta_wait(x)

    for w in range(2):
        for route in range(2):
            z_copy(1, w, route, 1).start()

    for h in range(2):
        d_copy(0, h).start()

    def u_cols(zh_, c_):
        return up_map.at[0, :, pl.ds(pl.multiple_of(((x * 2 + zh_) * 2 + c_) * 384, 128), 384)]

    def u_local(zh_):
        return pltpu.make_async_copy(u_cols(zh_, c), ub.at[c, zh_], u_s.at[2 + zh_])

    def u_copy(zh_):
        return rcopy(u_cols(zh_, 1 - c), ub.at[c, zh_], u_s.at[zh_], u_r.at[zh_], twin)

    for zh_ in range(2):
        u_local(zh_).start()
        u_copy(zh_).start()

    def y_stage(s, j):
        for way in range(2):
            by_wait(s, j, way)
            bo_copy(s, j, way).start()

    def step(k, _):
        for w in range(2):
            for route in range(2):
                z_wait(0, w, route, k)
                z_copy(0, w, route, k + 1).start()
        for route in range(2):
            for way in range(2):
                by_copy(-k if route == 0 else k, 2 * k - 1 + route, way).start()
        for w in range(2):
            for route in range(2):
                z_wait(1, w, route, k)
                z_copy(1, w, route, k + 1).start()
        for route in range(2):
            s = -(k - 1) if route == 0 else (k - 1)

            @pl.when((k > 1) | (route == 0))
            def _():
                y_stage(s, jnp.where(k == 1, 0, 2 * k - 3 + route))
        return 0

    lax.fori_loop(1, 4, step, 0)
    t_wait(0)
    t_copy(4).start()
    d_copy(1, 0).start()
    t_wait(2)
    t_copy(5).start()
    d_copy(2, 1).start()
    lax.fori_loop(4, 7, step, 0)
    t_wait(1)
    d_copy(1, 1).start()
    t_wait(3)
    d_copy(2, 0).start()
    for w in range(2):
        for route in range(2):
            z_wait(0, w, route, 7)
            if route == w:
                z_copy(0, w, route, 8).start()
    for route in range(2):
        for way in range(2):
            by_copy(-7 if route == 0 else 7, 13 + route, way).start()
    for w in range(2):
        for route in range(2):
            z_wait(1, w, route, 7)
            if route == w:
                z_copy(1, w, route, 8).start()
    y_stage(-6, 11)
    y_stage(6, 12)
    for w in range(2):
        z_wait(0, w, w, 8)
    for way in range(3):
        by_last(way).start()
    y_stage(-7, 13)
    y_stage(7, 14)
    for i in (4, 5):
        t_wait(i)
        d_copy(3, i - 4).start()
    for w in range(2):
        z_wait(1, w, w, 8)
    for way in range(3):
        by_last_wait(way)

    def bo_step(j, _):
        s = jnp.where(j % 2 == 1, -((j + 1) // 2), (j + 1) // 2)
        for way in range(2):
            bo_wait(s, j, way)
        return 0

    for way in range(2):
        bo_wait(0, 0, way)
    lax.fori_loop(1, 15, bo_step, 0)
    for r in range(4):
        for h in range(2):
            d_wait(r, h)
    for zh_ in range(2):
        u_local(zh_).wait()
        rcopy(ub.at[1 - c, zh_], ub.at[1 - c, zh_], u_s.at[zh_], u_r.at[zh_], twin).wait_recv()

    def member(m, _):
        lo = tok[:, m, :, LOW : LOW + 128].reshape(4 * ROWS, 128)
        for b in range(4):
            zh_, is_b = b // 2, b % 2
            c0, c1 = (128, 384) if is_b else (0, 128)
            if is_b:
                wi, wo = wb[zh_, 0].reshape(D, 256), wb[zh_, 1].reshape(D, 256)
            else:
                wi, wo = wa[zh_, 0].reshape(D, 128), wa[zh_, 1].reshape(D, 128)
            u = ub[m, zh_, :, c0:c1]
            pre = dot(tok[:, m, :, 0:D].reshape(4 * ROWS, D), wi) + dot(lo[:, 0:RANK], u)
            dhid = 0.5 * dot(tok[:, m, :, COT:WIDE].reshape(4 * ROWS, D), wo)
            sig = jax.nn.sigmoid(pre)
            dpre = (dhid * sig * (1.0 + pre * (1.0 - sig))).astype(BF16)
            part = dot(lo, dpre, ((0,), (0,)))
            for r in range(8):
                rss[m, r, :, zh_ * 384 + c0 : zh_ * 384 + c1] = part[8 * r : 8 * r + 8].astype(BF16)
            for x_ in range(4):
                bp = dot(u, dpre[ROWS * x_ : ROWS * (x_ + 1)], ((1,), (1,)))
                if b == 0:
                    bks[x_, m] = bp
                else:
                    bks[x_, m] += bp
        return 0

    lax.fori_loop(0, 2, member, 0)

    def bk_copy(d, c_):
        x_ = (x + d) % 4
        return rcopy(bks.at[x_, c_], bkr.at[x, c], bk_s.at[d, c_], bk_r.at[d, c], dev(x_, y, z, c_))

    def bk_other():
        return rcopy(bks.at[x, 1 - c], bkr.at[x, c], bk_s.at[0, 0], bk_r.at[0, 0], twin)

    bk_other().start()
    for d in range(1, 4):
        for c_ in range(2):
            bk_copy(d, c_).start()

    def rs_copy(d, c_):
        return rcopy(rss.at[c_, (zl + d) % 8], rsr.at[zl, c], rs_s.at[d, c_], rs_r.at[d, c], zdev(d, c_))

    def rs_other():
        return rcopy(rss.at[1 - c, zl], rsr.at[zl, c], rs_s.at[0, 0], rs_r.at[0, 0], twin)

    rs_other().start()
    for d in range(1, 8):
        for c_ in range(2):
            rs_copy(d, c_).start()
    rsr[zl, c] = rss[c, zl]
    bkr[x, c] = bks[x, c]

    rcopy(bkr.at[x, 1 - c], bkr.at[x, 1 - c], bk_s.at[0, 0], bk_r.at[0, 0], twin).wait_recv()
    for d in range(1, 4):
        for c_ in range(2):
            slot = bkr.at[(x + 4 - d) % 4, c_]
            rcopy(slot, slot, bk_s.at[d, c_], bk_r.at[d, c_], twin).wait_recv()
    total = bkr[0, 0]
    for i in range(1, 8):
        total = total + bkr[i // 2, i % 2]
    bka[x] = total.astype(BF16)

    def ba_copy(d):
        return rcopy(bka.at[x], bka.at[x], ba_s.at[d], ba_r.at[d], dev((x + d) % 4, y, z, c))

    for d in range(1, 4):
        ba_copy(d).start()
    for d in range(1, 4):
        slot = bka.at[(x + 4 - d) % 4]
        rcopy(slot, slot, ba_s.at[d], ba_r.at[d], right).wait_recv()
    quarter = pl.ds(pl.multiple_of(x * 384, 128), 384)
    part = dot(bka[0], tok[0, c, :, quarter])
    for x_ in range(1, 4):
        part = part + dot(bka[x_], tok[x_, c, :, quarter])
    for r in range(8):
        dns[r] = part[8 * r : 8 * r + 8].astype(BF16)

    def dn_copy(d):
        return rcopy(dns.at[(zl + d) % 8], dnr.at[zl], dn_s.at[d], dn_r.at[d], zdev(d, c))

    for d in range(1, 8):
        dn_copy(d).start()
    dnr[zl] = dns[zl]

    other = rsr.at[zl, 1 - c]
    rcopy(other, other, rs_s.at[0, 0], rs_r.at[0, 0], twin).wait_recv()
    for d in range(1, 8):
        for c_ in range(2):
            slot = rsr.at[(zl + 8 - d) % 8, c_]
            rcopy(slot, slot, rs_s.at[d, c_], rs_r.at[d, c_], twin).wait_recv()
    for c_ in range(2):
        total = rsr[0, c_].astype(F32)
        for i in range(1, 8):
            total = total + rsr[i, c_].astype(F32)
        ag[x, zl, :, 768 * c_ : 768 * (c_ + 1)] = total.astype(BF16)
    for d in range(1, 8):
        slot = dnr.at[(zl + 8 - d) % 8]
        rcopy(slot, slot, dn_s.at[d], dn_r.at[d], twin).wait_recv()
    total = dnr[0].astype(F32)
    for i in range(1, 8):
        total = total + dnr[i].astype(F32)
    ag[x, zl, :, 1536:1920] = total.astype(BF16)

    def gz_copy(d):
        return rcopy(ag.at[x, zl], ag.at[x, zl], gz_s.at[d], gz_r.at[d], zdev(d, c))

    for d in range(1, 8):
        gz_copy(d).start()
    for d in range(1, 8):
        slot = ag.at[x, (zl + 8 - d) % 8]
        rcopy(slot, slot, gz_s.at[d], gz_r.at[d], right).wait_recv()

    def g_half(x_, h):
        return ag.at[x_, pl.ds(4 * h, 4)]

    def gx_copy(i):
        x_, h, to = [
            (x, 0, right), (x, 1, right), (x, 1, left), (x, 0, left), (xl, 0, right), (xr, 1, left)
        ][i]
        return rcopy(g_half(x_, h), g_half(x_, h), gx_s.at[i], gx_r.at[i], to)

    def gx_wait(i):
        x_, h = [(xl, 0), (xl, 1), (xr, 1), (xr, 0), (xo, 0), (xo, 1)][i]
        rcopy(g_half(x_, h), g_half(x_, h), gx_s.at[i], gx_r.at[i], right).wait_recv()

    for i in (0, 2, 1, 3):
        gx_copy(i).start()
    gx_wait(0)
    gx_copy(4).start()
    gx_wait(2)
    gx_copy(5).start()
    for i in (1, 3, 4, 5):
        gx_wait(i)

    @pl.when(x != y)
    def _():
        tb_copy().wait_send()
        ta_copy(0).wait_send()

    for e in range(1, 4):
        ta_copy(e).wait_send()
    for i in range(6):
        t_copy(i).wait_send()
        gx_copy(i).wait_send()
    for r in range(4):
        for h in range(2):
            d_copy(r, h).wait_send()
    for zh_ in range(2):
        u_copy(zh_).wait_send()
    for route in range(2):
        def z_sent(k, _):
            for w in range(2):
                for i in range(2):
                    z_copy(i, w, route, k).wait_send()
            return 0

        lax.fori_loop(1, 8, z_sent, 0)
        for i in range(2):
            z_copy(i, route, route, 8).wait_send()

        def y_sent(j, _):
            by_copy(0, j, route).wait_send()
            bo_copy(0, j, route).wait_send()
            return 0

        lax.fori_loop(0, 15, y_sent, 0)
    for way in range(3):
        by_last(way).wait_send()
    bk_other().wait_send()
    rs_other().wait_send()
    for c_ in range(2):
        for d in range(1, 4):
            bk_copy(d, c_).wait_send()
        for d in range(1, 8):
            rs_copy(d, c_).wait_send()
    for d in range(1, 4):
        ba_copy(d).wait_send()
    for d in range(1, 8):
        dn_copy(d).wait_send()
        gz_copy(d).wait_send()


def spread(ag, dn_out, up_out):
    def write(i, _):
        rows = pl.ds(pl.multiple_of(8 * i, 8), 8)
        for x_ in range(4):
            for c_ in range(2):
                for h in range(2):
                    col = ((x_ * 2 + h) * 2 + c_) * 384
                    src = 768 * c_ + 384 * h
                    up_out[rows, col : col + 384] = ag[x_, i, :, src : src + 384].astype(F32)
            dn_out[rows, 384 * x_ : 384 * (x_ + 1)] = ag[x_, i, :, 1536:1920].astype(F32)
        return 0

    lax.fori_loop(0, 8, write, 0)


def on_device(frames, gain, w1, w2, down_map, up_map, lengths, cot):
    vmem = pl.BlockSpec(memory_space=pltpu.VMEM)
    dma = pltpu.SemaphoreType.DMA
    pieces = pl.pallas_call(
        kernel,
        out_shape=jax.ShapeDtypeStruct((4, 8, 8, 1920), BF16),
        in_specs=[vmem, vmem, vmem, vmem, vmem, pl.BlockSpec(memory_space=pl.ANY),
                  pl.BlockSpec(memory_space=pltpu.SMEM), vmem],
        out_specs=vmem,
        scratch_shapes=[
            pltpu.VMEM((2, 48, 128), BF16),
            pltpu.VMEM((2, 48, 256), BF16),
            pltpu.VMEM((2, 2, 4, 8, 48, 128), BF16),
            pltpu.VMEM((2, 2, 4, 8, 48, 256), BF16),
            pltpu.VMEM((4, 2, ROWS, WIDE), BF16),
            pltpu.VMEM((2, 2, RANK, 384), BF16),
            pltpu.VMEM((4, 2, RANK, ROWS), F32),
            pltpu.VMEM((4, 2, RANK, ROWS), F32),
            pltpu.VMEM((4, RANK, ROWS), BF16),
            pltpu.VMEM((2, 8, 8, 768), BF16),
            pltpu.VMEM((8, 2, 8, 768), BF16),
            pltpu.VMEM((8, 8, 384), BF16),
            pltpu.VMEM((8, 8, 384), BF16),
            dma((4,)), dma((4,)), dma((1,)), dma((1,)), dma((6,)), dma((6,)), dma((8,)), dma((8,)), dma((4,)), dma((2,)),
            dma((2, 2, 9)), dma((2, 2, 9)), dma((2, 2, 9)), dma((2, 2, 9)),
            dma((3, 16)), dma((3, 16)), dma((2, 16)), dma((2, 16)),
            dma((4, 2)), dma((4, 2)), dma((4,)), dma((4,)), dma((8, 2)), dma((8, 2)),
            dma((8,)), dma((8,)), dma((8,)), dma((8,)), dma((6,)), dma((6,)),
        ],
        compiler_params=pltpu.CompilerParams(
            collective_id=0, has_side_effects=True, vmem_limit_bytes=56 * 1024 * 1024
        ),
    )(frames, gain, w1, w2.T, down_map[0].T, up_map, lengths, cot)
    dn, up = pl.pallas_call(
        spread,
        out_shape=(
            jax.ShapeDtypeStruct((RANK, D), F32),
            jax.ShapeDtypeStruct((RANK, 6144), F32),
        ),
        in_specs=[vmem],
        out_specs=(vmem, vmem),
    )(pieces)
    return dn.T[None], up[None]


def solution(mesh):
    in_specs = (
        P("member", "fsdp", None),
        P(),
        P("fsdp", "member"),
        P("member", "fsdp"),
        P("member", None, None),
        P("member", None, None),
        P("member", "fsdp"),
        P("member", "fsdp", None),
    )
    out_specs = (P("member", None, None), P("member", None, None))
    return jax.shard_map(
        on_device, mesh=mesh, in_specs=in_specs, out_specs=out_specs, check_vma=False
    )
```

```python
import jax
import jax.numpy as jnp
from jax import lax
from jax.experimental import pallas as pl
from jax.experimental.pallas import tpu as pltpu
from jax.sharding import PartitionSpec as P

MESH = pl.DeviceIdType.MESH
ROWS = 128
D = 1536
RANK = 64
LOW = D
COT = D + 128
WIDE = 2 * D + 128
F32 = jnp.float32
BF16 = jnp.bfloat16


def dot(a, b, dims=((1,), (0,))):
    return lax.dot_general(a, b, (dims, ((), ())), preferred_element_type=F32)


def kernel(
    frames, gain, w1, w2t, down_map, up_map, lengths, cot,
    agu, agd,
    ws_a, ws_b, wa, wb, tok, ub, bks, bkr, bka, rss, rsr, dns, dnr,
    ta_s, ta_r, tb_s, tb_r, tk_s, tk_r, td_s, td_r, u_s, u_r,
    az_s, az_r, bz_s, bz_r, by_s, by_r, bo_s, bo_r,
    bk_s, bk_r, ba_s, ba_r, rs_s, rs_r, dn_s, dn_r, gz_s, gz_r, gx_s, gx_r,
):
    fi = lax.axis_index("fsdp")
    mi = lax.axis_index("member")
    x, zl = fi // 8, fi % 8
    y, zh, c = mi // 4, (mi // 2) % 2, mi % 2
    z = zh * 8 + zl

    def dev(x_, y_, z_, c_):
        return (x_ * 8 + z_ % 8, y_ * 4 + (z_ // 8) * 2 + c_)

    xr, xl, xo = (x + 1) % 4, (x + 3) % 4, (x + 2) % 4
    yr, yl, yo = (y + 1) % 4, (y + 3) % 4, (y + 2) % 4
    right, left = dev(xr, y, z, c), dev(xl, y, z, c)
    up, dn = dev(x, yr, z, c), dev(x, yl, z, c)
    fore, aft = dev(x, y, (z + 1) % 16, c), dev(x, y, (z + 15) % 16, c)
    twin = dev(x, y, z, 1 - c)
    flip = dev(y, x, z, c)

    def zdev(d, c_):
        return dev(x, y, zh * 8 + (zl + d) % 8, c_)

    def rcopy(src, dst, ss, rs, to):
        return pltpu.make_async_remote_copy(
            src_ref=src, dst_ref=dst, send_sem=ss, recv_sem=rs, device_id=to, device_id_type=MESH
        )

    def sent(ref, sem):
        rcopy(ref, ref, sem, sem, right).wait_send()

    def got(ref, sem):
        rcopy(ref, ref, sem, sem, right).wait_recv()

    barrier = pltpu.get_barrier_semaphore()
    peers = [up, dn, dev(x, yo, z, c), fore, aft, twin]
    for d in range(1, 4):
        for c_ in range(2):
            peers.append(dev((x + d) % 4, y, z, c_))
    for d in range(1, 8):
        for c_ in range(2):
            peers.append(zdev(d, c_))
    for peer in peers:
        pl.semaphore_signal(barrier, inc=1, device_id=peer, device_id_type=MESH)

    for e in range(1, 4):
        peer = dev((x + e) % 4, x, z, c)
        pl.semaphore_signal(barrier, inc=1, device_id=peer, device_id_type=MESH)

    @pl.when(x != y)
    def _():
        pl.semaphore_signal(barrier, inc=1, device_id=dev(x, x, z, c), device_id_type=MESH)
        pl.semaphore_signal(barrier, inc=1, device_id=flip, device_id_type=MESH)

    ws_a[0] = w1[:, 0:128]
    ws_b[0] = w1[:, 128:384]
    ws_a[1] = w2t[:, 0:128]
    ws_b[1] = w2t[:, 128:384]

    pl.semaphore_wait(barrier, len(peers) + jnp.where(x != y, 5, 3))

    def ta_copy(e):
        to = dev(y, (y + e) % 4, z, c)
        return rcopy(ws_a, wa.at[zh, :, x, zl], ta_s.at[e], ta_r.at[x], to)

    def ta_wait(a):
        slot = wa.at[zh, :, a, zl]
        rcopy(slot, slot, ta_s.at[0], ta_r.at[a], flip).wait_recv()

    def tb_copy():
        return rcopy(ws_b, wb.at[zh, :, x, zl], tb_s.at[0], tb_r.at[0], flip)

    @pl.when(x != y)
    def _():
        tb_copy().start()
        ta_copy(0).start()

    @pl.when(x == y)
    def _():
        for w in range(2):
            wa[zh, w, y, zl] = ws_a[w]
            wb[zh, w, y, zl] = ws_b[w]

    for e in range(1, 4):
        ta_copy(e).start()

    v = frames[0, 0:ROWS, :].astype(F32)
    mean = jnp.mean(v, axis=1, keepdims=True)
    var = jnp.mean((v - mean) ** 2, axis=1, keepdims=True)
    normed = (gain[...][None, :] * (v - mean) / jnp.sqrt(var + 1e-05)).astype(BF16)
    low = dot(normed, down_map[...], ((1,), (1,))).astype(BF16)
    keep = lax.broadcasted_iota(jnp.int32, (ROWS, D), 0) < lengths[0, 0]
    masked = jnp.where(keep, cot[0, 0:ROWS, :].astype(F32), 0.0).astype(BF16)
    tok[x, c, :, 0:D] = normed
    tok[x, c, :, LOW : LOW + 128] = jnp.concatenate([low, jnp.zeros_like(low)], axis=1)
    tok[x, c, :, COT:WIDE] = masked

    def half(x_, h):
        return tok.at[x_, c, pl.ds(64 * h, 64), :]

    def halfo(x_, h):
        return tok.at[x_, 1 - c, pl.ds(64 * h, 64), :]

    def t_copy(i):
        x_, h, to = [
            (x, 0, right), (x, 1, right), (x, 1, left), (x, 0, left), (xl, 0, right), (xr, 1, left)
        ][i]
        return rcopy(half(x_, h), half(x_, h), tk_s.at[0], tk_r.at[i], to)

    def t_wait(i):
        x_, h = [(xl, 0), (xl, 1), (xr, 1), (xr, 0), (xo, 0), (xo, 1)][i]
        got(half(x_, h), tk_r.at[i])

    def d_copy(r, h):
        x_ = [x, xl, xr, xo][r]
        return rcopy(half(x_, h), half(x_, h), td_s.at[0], td_r.at[0], twin)

    for i in (0, 2, 1, 3):
        t_copy(i).start()

    def a_str(s, w):
        z_ = (z + s + 16) % 16
        return wa.at[z_ // 8, w, :, z_ % 8]

    def b_str(s, w):
        return b_half(s, y, w)

    def b_blk(s, y_):
        z_ = (z + s + 16) % 16
        return wb.at[z_ // 8, :, y_, z_ % 8]

    def b_half(s, y_, w):
        z_ = (z + s + 16) % 16
        return wb.at[z_ // 8, w, y_, z_ % 8]

    streams = [(b_str, bz_s, bz_r), (a_str, az_s, az_r)]

    def z_copy(i, w, route, k):
        make, ss, rs = streams[i]
        blk = make((-(k - 1)) if route == 0 else (k - 1), w)
        return rcopy(blk, blk, ss.at[route], rs.at[route, w, k - 1], fore if route == 0 else aft)

    def z_wait(i, w, route, k):
        make, ss, rs = streams[i]
        blk = make(-k if route == 0 else k, w)
        got(blk, rs.at[route, w, k - 1])

    def by_copy(s, j, way):
        return rcopy(b_blk(s, y), b_blk(s, y), by_s.at[way], by_r.at[way, j], up if way == 0 else dn)

    def by_wait(s, j, way):
        y_ = yl if way == 0 else yr
        got(b_blk(s, y_), by_r.at[way, j])

    def by_last(way):
        blk = b_blk(8, y)
        return rcopy(blk, blk, by_s.at[way], by_r.at[way, 15], [up, dn, dev(x, yo, z, c)][way])

    def by_last_wait(way):
        blk = b_blk(8, [yl, yr, yo][way])
        got(blk, by_r.at[way, 15])

    def bo_copy(s, way):
        y_ = yl if way == 0 else yr
        return rcopy(
            b_half(s, y_, way), b_half(s, y_, way), bo_s.at[way], bo_r.at[way], up if way == 0 else dn
        )

    @pl.when(x != y)
    def _():
        blk = wb.at[zh, :, y, zl]
        rcopy(blk, blk, tb_s.at[0], tb_r.at[0], flip).wait_recv()

    for w in range(2):
        for route in range(2):
            z_copy(0, w, route, 1).start()
    for way in range(2):
        by_copy(0, 0, way).start()
    for e in range(1, 4):
        ta_wait((x + e) % 4)

    @pl.when(x != y)
    def _():
        ta_wait(x)

    for w in range(2):
        for route in range(2):
            z_copy(1, w, route, 1).start()

    for h in range(2):
        d_copy(0, h).start()

    def u_cols(zh_, c_):
        return up_map.at[0, :, pl.ds(pl.multiple_of(((x * 2 + zh_) * 2 + c_) * 384, 128), 384)]

    def u_local(zh_):
        return pltpu.make_async_copy(u_cols(zh_, c), ub.at[c, zh_], u_s.at[2 + zh_])

    def u_copy(zh_):
        return rcopy(u_cols(zh_, 1 - c), ub.at[c, zh_], u_s.at[zh_], u_r.at[zh_], twin)

    for zh_ in range(2):
        u_local(zh_).start()
        u_copy(zh_).start()

    def y_stage(s, j):
        for way in range(2):
            by_wait(s, j, way)
            bo_copy(s, way).start()

    def step(k, _):
        for w in range(2):
            for route in range(2):
                z_wait(0, w, route, k)
                z_copy(0, w, route, k + 1).start()
        for route in range(2):
            for way in range(2):
                by_copy(-k if route == 0 else k, 2 * k - 1 + route, way).start()
        for w in range(2):
            for route in range(2):
                z_wait(1, w, route, k)
                z_copy(1, w, route, k + 1).start()
        for route in range(2):
            s = -(k - 1) if route == 0 else (k - 1)

            @pl.when((k > 1) | (route == 0))
            def _():
                y_stage(s, jnp.where(k == 1, 0, 2 * k - 3 + route))
        return 0

    lax.fori_loop(1, 4, step, 0)
    t_wait(0)
    t_copy(4).start()
    d_copy(1, 0).start()
    t_wait(2)
    t_copy(5).start()
    d_copy(2, 1).start()
    lax.fori_loop(4, 7, step, 0)
    t_wait(1)
    d_copy(1, 1).start()
    t_wait(3)
    d_copy(2, 0).start()
    for w in range(2):
        for route in range(2):
            z_wait(0, w, route, 7)
            if route == w:
                z_copy(0, w, route, 8).start()
    for route in range(2):
        for way in range(2):
            by_copy(-7 if route == 0 else 7, 13 + route, way).start()
    for w in range(2):
        for route in range(2):
            z_wait(1, w, route, 7)
            if route == w:
                z_copy(1, w, route, 8).start()
    y_stage(-6, 11)
    y_stage(6, 12)
    for w in range(2):
        z_wait(0, w, w, 8)
    for way in range(3):
        by_last(way).start()
    y_stage(-7, 13)
    y_stage(7, 14)
    for i in (4, 5):
        t_wait(i)
        d_copy(3, i - 4).start()
    for w in range(2):
        z_wait(1, w, w, 8)
    for way in range(3):
        by_last_wait(way)

    for way in range(2):
        got(wb.at[0, 0, 0:3, 0:5], bo_r.at[way])
    got(tok.at[:, 0], td_r.at[0])
    for zh_ in range(2):
        u_local(zh_).wait()
        rcopy(ub.at[1 - c, zh_], ub.at[1 - c, zh_], u_s.at[zh_], u_r.at[zh_], twin).wait_recv()

    def half_of(zh_):
        def member(m, _):
            lo = tok[:, m, :, LOW : LOW + 128].reshape(4 * ROWS, 128)
            for is_b in range(2):
                c0, c1 = (128, 384) if is_b else (0, 128)
                if is_b:
                    wi, wo = wb[zh_, 0].reshape(D, 256), wb[zh_, 1].reshape(D, 256)
                else:
                    wi, wo = wa[zh_, 0].reshape(D, 128), wa[zh_, 1].reshape(D, 128)
                u = ub[m, zh_, :, c0:c1]
                pre = dot(tok[:, m, :, 0:D].reshape(4 * ROWS, D), wi) + dot(lo[:, 0:RANK], u)
                dhid = 0.5 * dot(tok[:, m, :, COT:WIDE].reshape(4 * ROWS, D), wo)
                sig = jax.nn.sigmoid(pre)
                dpre = (dhid * sig * (1.0 + pre * (1.0 - sig))).astype(BF16)
                part = dot(lo, dpre, ((0,), (0,)))
                for r in range(8):
                    rss[zh_, m, r, :, c0:c1] = part[8 * r : 8 * r + 8].astype(BF16)
                for x_ in range(4):
                    bp = dot(u, dpre[ROWS * x_ : ROWS * (x_ + 1)], ((1,), (1,)))
                    if zh_ == 0 and is_b == 0:
                        bks[x_, m] = bp
                    else:
                        bks[x_, m] += bp
            return 0

        lax.fori_loop(0, 2, member, 0)

    def rs_copy(g, d, c_):
        return rcopy(
            rss.at[g, c_, (zl + d) % 8], rsr.at[g, zl, c], rs_s.at[g, c_], rs_r.at[g, c], zdev(d, c_)
        )

    def rs_other(g):
        return rcopy(rss.at[g, 1 - c, zl], rsr.at[g, zl, c], rs_s.at[g, 2], rs_r.at[g, 2], twin)

    def rs_start(g):
        for d in (4, 3, 5, 2, 6, 1, 7):
            for c_ in range(2):
                rs_copy(g, d, c_).start()
        rs_other(g).start()
        rsr[g, zl, c] = rss[g, c, zl]

    def rs_sum(g):
        got(rsr.at[g, zl, 1 - c], rs_r.at[g, 2])
        for c_ in range(2):
            got(rsr.at[g, 0:7, c_], rs_r.at[g, c_])
        for c_ in range(2):
            total = rsr[g, 0, c_].astype(F32)
            for i in range(1, 8):
                total = total + rsr[g, i, c_].astype(F32)
            agu[g, x, zl, :, 384 * c_ : 384 * (c_ + 1)] = total.astype(BF16)

    def bk_copy(d, c_):
        x_ = (x + d) % 4
        return rcopy(bks.at[x_, c_], bkr.at[x, c], bk_s.at[c_], bk_r.at[c], dev(x_, y, z, c_))

    def bk_other():
        return rcopy(bks.at[x, 1 - c], bkr.at[x, c], bk_s.at[2], bk_r.at[2], twin)

    def ba_copy(d):
        return rcopy(bka.at[x], bka.at[x], ba_s.at[0], ba_r.at[0], dev((x + d) % 4, y, z, c))

    def dn_copy(d):
        return rcopy(dns.at[(zl + d) % 8], dnr.at[zl], dn_s.at[0], dn_r.at[0], zdev(d, c))

    z4, q4 = (zl // 4) * 4, zl % 4
    far = (zl + 4) % 8

    def piece(g, zl_):
        return agd.at[x, zl_] if g == 2 else agu.at[g, x, zl_]

    def near(j):
        return dev(x, y, zh * 8 + z4 + (q4 + j) % 4, c)

    def gz_copy(g, j):
        if j == 0:
            return rcopy(piece(g, zl), piece(g, zl), gz_s.at[g], gz_r.at[g, 0], dev(x, y, zh * 8 + far, c))
        src = zl if j < 4 else far
        return rcopy(piece(g, src), piece(g, src), gz_s.at[g], gz_r.at[g, 1 if j < 4 else 2], near((j - 1) % 3 + 1))

    def gz_wait(g, i):
        slots = agd.at[0] if g == 2 else agu.at[g, 0]
        got(slots.at[0:1] if i == 0 else slots.at[0:3], gz_r.at[g, i])

    def g_half(g, x_, h):
        return agu.at[g, x_, pl.ds(z4 if h == 0 else 4 - z4, 4)]

    def gx_copy(g, i):
        x_, h, to = [
            (x, 0, right), (x, 1, right), (x, 1, left), (x, 0, left), (xl, 0, right), (xr, 1, left)
        ][i]
        return rcopy(g_half(g, x_, h), g_half(g, x_, h), gx_s.at[g], gx_r.at[g, i], to)

    def gx_wait(g, i):
        x_, h = [(xl, 0), (xl, 1), (xr, 1), (xr, 0), (xo, 0), (xo, 1)][i]
        got(g_half(g, x_, h), gx_r.at[g, i])

    def gd_copy(d):
        return rcopy(agd.at[x], agd.at[x], gx_s.at[2], gx_r.at[2, 0], dev((x + d) % 4, y, z, c))

    def gz_own(g):
        for j in range(4):
            gz_copy(g, j).start()

    def gz_pass(g):
        gz_wait(g, 0)
        for j in range(4, 7):
            gz_copy(g, j).start()

    def gx_first(g):
        gz_wait(g, 1)
        gx_copy(g, 0).start()
        gx_copy(g, 3).start()

    def gx_second(g):
        gz_wait(g, 2)
        gx_copy(g, 2).start()
        gx_copy(g, 1).start()

    def gx_pass(g):
        gx_wait(g, 0)
        gx_copy(g, 4).start()
        gx_wait(g, 2)
        gx_copy(g, 5).start()

    half_of(0)
    rs_start(0)
    half_of(1)
    for d in range(1, 4):
        for c_ in range(2):
            bk_copy(d, c_).start()
    bk_other().start()
    rs_start(1)
    bkr[x, c] = bks[x, c]

    got(bkr.at[x, 1 - c], bk_r.at[2])
    for c_ in range(2):
        got(bkr.at[0:3, c_], bk_r.at[c_])
    total = bkr[0, 0]
    for i in range(1, 8):
        total = total + bkr[i // 2, i % 2]
    bka[x] = total.astype(BF16)
    for d in range(1, 4):
        ba_copy(d).start()

    rs_sum(0)
    gz_own(0)

    got(bka.at[0:3], ba_r.at[0])
    quarter = pl.ds(pl.multiple_of(x * 384, 128), 384)
    part = dot(bka[0], tok[0, c, :, quarter])
    for x_ in range(1, 4):
        part = part + dot(bka[x_], tok[x_, c, :, quarter])
    for r in range(8):
        dns[r] = part[8 * r : 8 * r + 8].astype(BF16)
    for d in range(1, 8):
        dn_copy(d).start()
    dnr[zl] = dns[zl]

    rs_sum(1)
    gz_own(1)
    gz_pass(0)
    gx_first(0)
    got(dnr.at[0:7], dn_r.at[0])
    total = dnr[0].astype(F32)
    for i in range(1, 8):
        total = total + dnr[i].astype(F32)
    agd[x, zl] = total.astype(BF16)
    gz_own(2)
    gz_pass(1)
    gx_second(0)
    gx_first(1)
    gz_pass(2)
    gx_pass(0)
    gx_second(1)
    gz_wait(2, 1)
    gz_wait(2, 2)
    for d in range(1, 4):
        gd_copy(d).start()
    gx_pass(1)
    for g in range(2):
        for i in (1, 3, 4, 5):
            gx_wait(g, i)
    got(agd.at[0:3], gx_r.at[2, 0])

    @pl.when(x != y)
    def _():
        tb_copy().wait_send()
        ta_copy(0).wait_send()

    for e in range(1, 4):
        ta_copy(e).wait_send()
    sent(tok.at[0:3, 0], tk_s.at[0])
    sent(tok.at[:, 0], td_s.at[0])
    for zh_ in range(2):
        u_copy(zh_).wait_send()
    for route in range(2):
        sent(wa.at[0:2, 0:2, 0:3, 0:5], az_s.at[route])
        sent(wb.at[0, 0, 0:3, 0:5], bz_s.at[route])
        sent(wb.at[0, 0], by_s.at[route])
        sent(wb.at[0, 0, 0:3, 0:5], bo_s.at[route])
    sent(wb.at[0, 0, 0, 0:2], by_s.at[2])
    bk_other().wait_send()
    for c_ in range(2):
        sent(bks.at[0:3, 0], bk_s.at[c_])
    sent(bka.at[0:3], ba_s.at[0])
    sent(dns.at[0:7], dn_s.at[0])
    for g in range(2):
        rs_other(g).wait_send()
        for c_ in range(2):
            sent(rss.at[g, c_, 0:7], rs_s.at[g, c_])
        sent(agu.at[g, 0, 0:7], gz_s.at[g])
        sent(agu.at[g, 0:3], gx_s.at[g])
    sent(agd.at[0, 0:7], gz_s.at[2])
    sent(agd.at[0:3], gx_s.at[2])


def spread(agu, agd, dn_out, up_out):
    def write(i, _):
        rows = pl.ds(pl.multiple_of(8 * i, 8), 8)
        for x_ in range(4):
            for c_ in range(2):
                for h in range(2):
                    col = ((x_ * 2 + h) * 2 + c_) * 384
                    up_out[rows, col : col + 384] = agu[h, x_, i, :, 384 * c_ : 384 * (c_ + 1)].astype(F32)
            dn_out[rows, 384 * x_ : 384 * (x_ + 1)] = agd[x_, i].astype(F32)
        return 0

    lax.fori_loop(0, 8, write, 0)


def on_device(frames, gain, w1, w2, down_map, up_map, lengths, cot):
    vmem = pl.BlockSpec(memory_space=pltpu.VMEM)
    dma = pltpu.SemaphoreType.DMA
    pieces = pl.pallas_call(
        kernel,
        out_shape=(
            jax.ShapeDtypeStruct((2, 4, 8, 8, 768), BF16),
            jax.ShapeDtypeStruct((4, 8, 8, 384), BF16),
        ),
        in_specs=[vmem, vmem, vmem, vmem, vmem, pl.BlockSpec(memory_space=pl.ANY),
                  pl.BlockSpec(memory_space=pltpu.SMEM), vmem],
        out_specs=(vmem, vmem),
        scratch_shapes=[
            pltpu.VMEM((2, 48, 128), BF16),
            pltpu.VMEM((2, 48, 256), BF16),
            pltpu.VMEM((2, 2, 4, 8, 48, 128), BF16),
            pltpu.VMEM((2, 2, 4, 8, 48, 256), BF16),
            pltpu.VMEM((4, 2, ROWS, WIDE), BF16),
            pltpu.VMEM((2, 2, RANK, 384), BF16),
            pltpu.VMEM((4, 2, RANK, ROWS), F32),
            pltpu.VMEM((4, 2, RANK, ROWS), F32),
            pltpu.VMEM((4, RANK, ROWS), BF16),
            pltpu.VMEM((2, 2, 8, 8, 384), BF16),
            pltpu.VMEM((2, 8, 2, 8, 384), BF16),
            pltpu.VMEM((8, 8, 384), BF16),
            pltpu.VMEM((8, 8, 384), BF16),
            dma((4,)), dma((4,)), dma((1,)), dma((1,)), dma((1,)), dma((6,)), dma((1,)), dma((1,)), dma((4,)), dma((2,)),
            dma((2,)), dma((2, 2, 8)), dma((2,)), dma((2, 2, 8)),
            dma((3,)), dma((3, 16)), dma((2,)), dma((2,)),
            dma((3,)), dma((3,)), dma((1,)), dma((1,)), dma((2, 3)), dma((2, 3)),
            dma((1,)), dma((1,)), dma((3,)), dma((3, 3)), dma((3,)), dma((3, 6)),
        ],
        compiler_params=pltpu.CompilerParams(
            collective_id=0, has_side_effects=True, vmem_limit_bytes=56 * 1024 * 1024
        ),
    )(frames, gain, w1, w2.T, down_map[0].T, up_map, lengths, cot)
    dn, up = pl.pallas_call(
        spread,
        out_shape=(
            jax.ShapeDtypeStruct((RANK, D), F32),
            jax.ShapeDtypeStruct((RANK, 6144), F32),
        ),
        in_specs=[vmem, vmem],
        out_specs=(vmem, vmem),
    )(*pieces)
    return dn.T[None], up[None]


def solution(mesh):
    in_specs = (
        P("member", "fsdp", None),
        P(),
        P("fsdp", "member"),
        P("member", "fsdp"),
        P("member", None, None),
        P("member", None, None),
        P("member", "fsdp"),
        P("member", "fsdp", None),
    )
    out_specs = (P("member", None, None), P("member", None, None))
    return jax.shard_map(
        on_device, mesh=mesh, in_specs=in_specs, out_specs=out_specs, check_vma=False
    )
```

```python
import jax
import jax.numpy as jnp
from jax import lax
from jax.experimental import pallas as pl
from jax.experimental.pallas import tpu as pltpu
from jax.sharding import PartitionSpec as P

MESH = pl.DeviceIdType.MESH
ROWS = 128
D = 1536
RANK = 64
LOW = D
COT = D + 128
WIDE = 2 * D + 128
F32 = jnp.float32
BF16 = jnp.bfloat16


def dot(a, b, dims=((1,), (0,))):
    return lax.dot_general(a, b, (dims, ((), ())), preferred_element_type=F32)


def kernel(
    frames, gain, w1, w2t, down_map, up_map, lengths, cot,
    agu, agd,
    ws_a, ws_b, wa, wb, tok, ub, bks, bkr, bka, rss, rsr, dns, dnr,
    ta_s, ta_r, tb_s, tb_r, tk_s, tk_r, td_s, td_r, u_s, u_r,
    az_s, az_r, bz_s, bz_r, by_s, by_r, bo_s, bo_r,
    bk_s, bk_r, ba_s, ba_r, rs_s, rs_r, dn_s, dn_r, gz_s, gz_r, gx_s, gx_r,
):
    fi = lax.axis_index("fsdp")
    mi = lax.axis_index("member")
    x, zl = fi // 8, fi % 8
    y, zh, c = mi // 4, (mi // 2) % 2, mi % 2
    z = zh * 8 + zl

    def dev(x_, y_, z_, c_):
        return (x_ * 8 + z_ % 8, y_ * 4 + (z_ // 8) * 2 + c_)

    xr, xl, xo = (x + 1) % 4, (x + 3) % 4, (x + 2) % 4
    yr, yl, yo = (y + 1) % 4, (y + 3) % 4, (y + 2) % 4
    right, left = dev(xr, y, z, c), dev(xl, y, z, c)
    up, dn = dev(x, yr, z, c), dev(x, yl, z, c)
    fore, aft = dev(x, y, (z + 1) % 16, c), dev(x, y, (z + 15) % 16, c)
    twin = dev(x, y, z, 1 - c)
    flip = dev(y, x, z, c)

    def zdev(d, c_):
        return dev(x, y, zh * 8 + (zl + d) % 8, c_)

    def rcopy(src, dst, ss, rs, to):
        return pltpu.make_async_remote_copy(
            src_ref=src, dst_ref=dst, send_sem=ss, recv_sem=rs, device_id=to, device_id_type=MESH
        )

    def sent(ref, sem):
        rcopy(ref, ref, sem, sem, right).wait_send()

    def got(ref, sem):
        rcopy(ref, ref, sem, sem, right).wait_recv()

    barrier = pltpu.get_barrier_semaphore()
    peers = [up, dn, dev(x, yo, z, c), fore, aft, twin]
    for d in range(1, 4):
        for c_ in range(2):
            peers.append(dev((x + d) % 4, y, z, c_))
    for d in range(1, 8):
        for c_ in range(2):
            peers.append(zdev(d, c_))
    for peer in peers:
        pl.semaphore_signal(barrier, inc=1, device_id=peer, device_id_type=MESH)

    for e in range(1, 4):
        peer = dev((x + e) % 4, x, z, c)
        pl.semaphore_signal(barrier, inc=1, device_id=peer, device_id_type=MESH)

    @pl.when(x != y)
    def _():
        pl.semaphore_signal(barrier, inc=1, device_id=dev(x, x, z, c), device_id_type=MESH)
        pl.semaphore_signal(barrier, inc=1, device_id=flip, device_id_type=MESH)

    ws_a[0] = w1[:, 0:128]
    ws_b[0] = w1[:, 128:384]
    ws_a[1] = w2t[:, 0:128]
    ws_b[1] = w2t[:, 128:384]

    pl.semaphore_wait(barrier, len(peers) + jnp.where(x != y, 5, 3))

    def lanes(zh_):
        return pl.ds(pl.multiple_of(zh_ * 128, 128), 128)

    def ta_copy(e):
        to = dev(y, (y + e) % 4, z, c)
        return rcopy(ws_a, wa.at[:, x, zl, :, lanes(zh)], ta_s.at[e], ta_r.at[x], to)

    def ta_wait(a):
        slot = wa.at[:, a, zl, :, lanes(zh)]
        rcopy(slot, slot, ta_s.at[0], ta_r.at[a], flip).wait_recv()

    def tb_copy():
        return rcopy(ws_b, wb.at[zh, :, x, zl], tb_s.at[0], tb_r.at[0], flip)

    @pl.when(x != y)
    def _():
        tb_copy().start()
        ta_copy(0).start()

    @pl.when(x == y)
    def _():
        for w in range(2):
            wa[w, y, zl, :, lanes(zh)] = ws_a[w]
            wb[zh, w, y, zl] = ws_b[w]

    for e in range(1, 4):
        ta_copy(e).start()

    v = frames[0, 0:ROWS, :].astype(F32)
    mean = jnp.mean(v, axis=1, keepdims=True)
    var = jnp.mean((v - mean) ** 2, axis=1, keepdims=True)
    normed = (gain[...][None, :] * (v - mean) / jnp.sqrt(var + 1e-05)).astype(BF16)
    low = dot(normed, down_map[...], ((1,), (1,))).astype(BF16)
    keep = lax.broadcasted_iota(jnp.int32, (ROWS, D), 0) < lengths[0, 0]
    masked = jnp.where(keep, cot[0, 0:ROWS, :].astype(F32), 0.0).astype(BF16)
    tok[x, c, :, 0:D] = normed
    tok[x, c, :, LOW : LOW + 128] = jnp.concatenate([low, jnp.zeros_like(low)], axis=1)
    tok[x, c, :, COT:WIDE] = masked

    def half(x_, h):
        return tok.at[x_, c, pl.ds(64 * h, 64), :]

    def halfo(x_, h):
        return tok.at[x_, 1 - c, pl.ds(64 * h, 64), :]

    def t_copy(i):
        x_, h, to = [
            (x, 0, right), (x, 1, right), (x, 1, left), (x, 0, left), (xl, 0, right), (xr, 1, left)
        ][i]
        return rcopy(half(x_, h), half(x_, h), tk_s.at[0], tk_r.at[i], to)

    def t_wait(i):
        x_, h = [(xl, 0), (xl, 1), (xr, 1), (xr, 0), (xo, 0), (xo, 1)][i]
        got(half(x_, h), tk_r.at[i])

    def d_copy(r, h):
        x_ = [x, xl, xr, xo][r]
        return rcopy(half(x_, h), half(x_, h), td_s.at[0], td_r.at[0], twin)

    for i in (0, 2, 1, 3):
        t_copy(i).start()

    def a_str(s, w):
        z_ = (z + s + 16) % 16
        return wa.at[w, :, z_ % 8, :, lanes(z_ // 8)]

    def b_str(s, w):
        return b_half(s, y, w)

    def b_blk(s, y_):
        z_ = (z + s + 16) % 16
        return wb.at[z_ // 8, :, y_, z_ % 8]

    def b_half(s, y_, w):
        z_ = (z + s + 16) % 16
        return wb.at[z_ // 8, w, y_, z_ % 8]

    streams = [(b_str, bz_s, bz_r), (a_str, az_s, az_r)]

    def z_copy(i, w, route, k):
        make, ss, rs = streams[i]
        blk = make((-(k - 1)) if route == 0 else (k - 1), w)
        return rcopy(blk, blk, ss.at[route], rs.at[route, w, k - 1], fore if route == 0 else aft)

    def z_wait(i, w, route, k):
        make, ss, rs = streams[i]
        blk = make(-k if route == 0 else k, w)
        got(blk, rs.at[route, w, k - 1])

    def by_copy(s, j, way):
        return rcopy(b_blk(s, y), b_blk(s, y), by_s.at[way], by_r.at[way, j], up if way == 0 else dn)

    def by_wait(s, j, way):
        y_ = yl if way == 0 else yr
        got(b_blk(s, y_), by_r.at[way, j])

    def by_last(way):
        blk = b_blk(8, y)
        return rcopy(blk, blk, by_s.at[way], by_r.at[way, 15], [up, dn, dev(x, yo, z, c)][way])

    def by_last_wait(way):
        blk = b_blk(8, [yl, yr, yo][way])
        got(blk, by_r.at[way, 15])

    def bo_copy(s, way):
        y_ = yl if way == 0 else yr
        return rcopy(
            b_half(s, y_, way), b_half(s, y_, way), bo_s.at[way], bo_r.at[way], up if way == 0 else dn
        )

    @pl.when(x != y)
    def _():
        blk = wb.at[zh, :, y, zl]
        rcopy(blk, blk, tb_s.at[0], tb_r.at[0], flip).wait_recv()

    for w in range(2):
        for route in range(2):
            z_copy(0, w, route, 1).start()
    for way in range(2):
        by_copy(0, 0, way).start()
    for e in range(1, 4):
        ta_wait((x + e) % 4)

    @pl.when(x != y)
    def _():
        ta_wait(x)

    for w in range(2):
        for route in range(2):
            z_copy(1, w, route, 1).start()

    for h in range(2):
        d_copy(0, h).start()

    def u_cols(zh_, c_):
        return up_map.at[0, :, pl.ds(pl.multiple_of(((x * 2 + zh_) * 2 + c_) * 384, 128), 384)]

    def u_local(zh_):
        return pltpu.make_async_copy(u_cols(zh_, c), ub.at[c, zh_], u_s.at[2 + zh_])

    def u_copy(zh_):
        return rcopy(u_cols(zh_, 1 - c), ub.at[c, zh_], u_s.at[zh_], u_r.at[zh_], twin)

    for zh_ in range(2):
        u_local(zh_).start()
        u_copy(zh_).start()

    def y_stage(s, j):
        for way in range(2):
            by_wait(s, j, way)
            bo_copy(s, way).start()

    def step(k, _):
        for w in range(2):
            for route in range(2):
                z_wait(0, w, route, k)
                z_copy(0, w, route, k + 1).start()
        for route in range(2):
            for way in range(2):
                by_copy(-k if route == 0 else k, 2 * k - 1 + route, way).start()
        for w in range(2):
            for route in range(2):
                z_wait(1, w, route, k)
                z_copy(1, w, route, k + 1).start()
        for route in range(2):
            s = -(k - 1) if route == 0 else (k - 1)

            @pl.when((k > 1) | (route == 0))
            def _():
                y_stage(s, jnp.where(k == 1, 0, 2 * k - 3 + route))
        return 0

    lax.fori_loop(1, 4, step, 0)
    t_wait(0)
    t_copy(4).start()
    d_copy(1, 0).start()
    t_wait(2)
    t_copy(5).start()
    d_copy(2, 1).start()
    lax.fori_loop(4, 7, step, 0)
    t_wait(1)
    d_copy(1, 1).start()
    t_wait(3)
    d_copy(2, 0).start()
    for w in range(2):
        for route in range(2):
            z_wait(0, w, route, 7)
            if route == w:
                z_copy(0, w, route, 8).start()
    for route in range(2):
        for way in range(2):
            by_copy(-7 if route == 0 else 7, 13 + route, way).start()
    for w in range(2):
        for route in range(2):
            z_wait(1, w, route, 7)
            if route == w:
                z_copy(1, w, route, 8).start()
    y_stage(-6, 11)
    y_stage(6, 12)
    for w in range(2):
        z_wait(0, w, w, 8)
    for way in range(3):
        by_last(way).start()
    y_stage(-7, 13)
    y_stage(7, 14)
    for i in (4, 5):
        t_wait(i)
        d_copy(3, i - 4).start()
    for w in range(2):
        z_wait(1, w, w, 8)
    for way in range(3):
        by_last_wait(way)

    for way in range(2):
        got(wb.at[0, 0, 0:3, 0:5], bo_r.at[way])
    got(tok.at[:, 0], td_r.at[0])
    for zh_ in range(2):
        u_local(zh_).wait()
        rcopy(ub.at[1 - c, zh_], ub.at[1 - c, zh_], u_s.at[zh_], u_r.at[zh_], twin).wait_recv()

    def third(g):
        def member(m, _):
            lo = tok[:, m, :, LOW : LOW + 128].reshape(4 * ROWS, 128)
            if g < 2:
                wi, wo = wb[g, 0].reshape(D, 256), wb[g, 1].reshape(D, 256)
                u = ub[m, g, :, 128:384]
            else:
                wi, wo = wa[0].reshape(D, 256), wa[1].reshape(D, 256)
                u = jnp.concatenate([ub[m, 0, :, 0:128], ub[m, 1, :, 0:128]], axis=1)
            pre = dot(tok[:, m, :, 0:D].reshape(4 * ROWS, D), wi) + dot(lo[:, 0:RANK], u)
            dhid = 0.5 * dot(tok[:, m, :, COT:WIDE].reshape(4 * ROWS, D), wo)
            sig = jax.nn.sigmoid(pre)
            dpre = (dhid * sig * (1.0 + pre * (1.0 - sig))).astype(BF16)
            part = dot(lo, dpre, ((0,), (0,)))
            for r in range(8):
                rss[g, m, r] = part[8 * r : 8 * r + 8].astype(BF16)
            for x_ in range(4):
                bp = dot(u, dpre[ROWS * x_ : ROWS * (x_ + 1)], ((1,), (1,)))
                if g == 0:
                    bks[x_, m] = bp
                else:
                    bks[x_, m] += bp
            return 0

        lax.fori_loop(0, 2, member, 0)

    def rs_copy(g, d, c_):
        return rcopy(
            rss.at[g, c_, (zl + d) % 8], rsr.at[g, zl, c], rs_s.at[g, c_], rs_r.at[g, c], zdev(d, c_)
        )

    def rs_other(g):
        return rcopy(rss.at[g, 1 - c, zl], rsr.at[g, zl, c], rs_s.at[g, 2], rs_r.at[g, 2], twin)

    def rs_start(g):
        for d in (4, 3, 5, 2, 6, 1, 7):
            for c_ in range(2):
                rs_copy(g, d, c_).start()
        rs_other(g).start()
        rsr[g, zl, c] = rss[g, c, zl]

    def rs_sum(g):
        got(rsr.at[g, zl, 1 - c], rs_r.at[g, 2])
        for c_ in range(2):
            got(rsr.at[g, 0:7, c_], rs_r.at[g, c_])
        for c_ in range(2):
            total = rsr[g, 0, c_].astype(F32)
            for i in range(1, 8):
                total = total + rsr[g, i, c_].astype(F32)
            agu[g, x, zl, :, 256 * c_ : 256 * (c_ + 1)] = total.astype(BF16)

    def bk_copy(d, c_):
        x_ = (x + d) % 4
        return rcopy(bks.at[x_, c_], bkr.at[x, c], bk_s.at[c_], bk_r.at[c], dev(x_, y, z, c_))

    def bk_other():
        return rcopy(bks.at[x, 1 - c], bkr.at[x, c], bk_s.at[2], bk_r.at[2], twin)

    def ba_copy(d):
        return rcopy(bka.at[x], bka.at[x], ba_s.at[0], ba_r.at[0], dev((x + d) % 4, y, z, c))

    def dn_copy(d):
        return rcopy(dns.at[(zl + d) % 8], dnr.at[zl], dn_s.at[0], dn_r.at[0], zdev(d, c))

    z4, q4 = (zl // 4) * 4, zl % 4
    far = (zl + 4) % 8

    def piece(g, zl_):
        return agd.at[x, zl_] if g == 3 else agu.at[g, x, zl_]

    def near(j):
        return dev(x, y, zh * 8 + z4 + (q4 + j) % 4, c)

    def gz_copy(g, j):
        if j == 0:
            return rcopy(piece(g, zl), piece(g, zl), gz_s.at[g], gz_r.at[g, 0], dev(x, y, zh * 8 + far, c))
        src = zl if j < 4 else far
        return rcopy(piece(g, src), piece(g, src), gz_s.at[g], gz_r.at[g, 1 if j < 4 else 2], near((j - 1) % 3 + 1))

    def gz_wait(g, i):
        got(agu.at[g, 0, 0:1] if i == 0 else agu.at[g, 0, 0:3], gz_r.at[g, i])

    def gz_all(g):
        for d in (4, 3, 5, 2, 6, 1, 7):
            rcopy(piece(g, zl), piece(g, zl), gz_s.at[g], gz_r.at[g, 0], zdev(d, c)).start()

    def gz_all_wait(g):
        got(agd.at[0, 0:7] if g == 3 else agu.at[g, 0, 0:7], gz_r.at[g, 0])

    def g_half(g, x_, h):
        return agu.at[g, x_, pl.ds(z4 if h == 0 else 4 - z4, 4)]

    def gx_copy(g, i):
        x_, h, to = [
            (x, 0, right), (x, 1, right), (x, 1, left), (x, 0, left), (xl, 0, right), (xr, 1, left)
        ][i]
        return rcopy(g_half(g, x_, h), g_half(g, x_, h), gx_s.at[g], gx_r.at[g, i], to)

    def gx_wait(g, i):
        x_, h = [(xl, 0), (xl, 1), (xr, 1), (xr, 0), (xo, 0), (xo, 1)][i]
        got(g_half(g, x_, h), gx_r.at[g, i])

    def gd_copy(d):
        return rcopy(agd.at[x], agd.at[x], gx_s.at[3], gx_r.at[3, 0], dev((x + d) % 4, y, z, c))

    def gz_own(g):
        for j in range(4):
            gz_copy(g, j).start()

    def gz_pass(g):
        gz_wait(g, 0)
        for j in range(4, 7):
            gz_copy(g, j).start()

    def gx_first(g):
        gz_wait(g, 1)
        gx_copy(g, 0).start()
        gx_copy(g, 3).start()

    def gx_second(g):
        gz_wait(g, 2)
        gx_copy(g, 2).start()
        gx_copy(g, 1).start()

    def gx_pass(g):
        gx_wait(g, 0)
        gx_copy(g, 4).start()
        gx_wait(g, 2)
        gx_copy(g, 5).start()

    third(0)
    rs_start(0)
    third(1)
    rs_start(1)
    third(2)
    for d in range(1, 4):
        for c_ in range(2):
            bk_copy(d, c_).start()
    bk_other().start()
    rs_start(2)
    bkr[x, c] = bks[x, c]

    got(bkr.at[x, 1 - c], bk_r.at[2])
    for c_ in range(2):
        got(bkr.at[0:3, c_], bk_r.at[c_])
    total = bkr[0, 0]
    for i in range(1, 8):
        total = total + bkr[i // 2, i % 2]
    bka[x] = total.astype(BF16)
    for d in range(1, 4):
        ba_copy(d).start()

    rs_sum(0)
    gz_own(0)
    rs_sum(1)
    gz_own(1)

    got(bka.at[0:3], ba_r.at[0])
    quarter = pl.ds(pl.multiple_of(x * 384, 128), 384)
    part = dot(bka[0], tok[0, c, :, quarter])
    for x_ in range(1, 4):
        part = part + dot(bka[x_], tok[x_, c, :, quarter])
    for r in range(8):
        dns[r] = part[8 * r : 8 * r + 8].astype(BF16)
    for d in range(1, 8):
        dn_copy(d).start()
    dnr[zl] = dns[zl]

    rs_sum(2)
    gz_all(2)
    gz_pass(0)
    gx_first(0)
    gz_pass(1)
    gx_first(1)
    gx_second(0)
    got(dnr.at[0:7], dn_r.at[0])
    total = dnr[0].astype(F32)
    for i in range(1, 8):
        total = total + dnr[i].astype(F32)
    agd[x, zl] = total.astype(BF16)
    gz_all(3)
    gx_second(1)
    gx_pass(0)
    gz_all_wait(2)
    for i in (0, 2, 3, 1):
        gx_copy(2, i).start()
    gx_pass(1)
    gz_all_wait(3)
    for d in range(1, 4):
        gd_copy(d).start()
    gx_pass(2)
    for g in range(3):
        for i in (1, 3, 4, 5):
            gx_wait(g, i)
    got(agd.at[0:3], gx_r.at[3, 0])

    @pl.when(x != y)
    def _():
        tb_copy().wait_send()
        ta_copy(0).wait_send()

    for e in range(1, 4):
        ta_copy(e).wait_send()
    sent(tok.at[0:3, 0], tk_s.at[0])
    sent(tok.at[:, 0], td_s.at[0])
    for zh_ in range(2):
        u_copy(zh_).wait_send()
    for route in range(2):
        sent(wa.at[0:2, 0:3, 0:5], az_s.at[route])
        sent(wb.at[0, 0, 0:3, 0:5], bz_s.at[route])
        sent(wb.at[0, 0], by_s.at[route])
        sent(wb.at[0, 0, 0:3, 0:5], bo_s.at[route])
    sent(wb.at[0, 0, 0, 0:2], by_s.at[2])
    bk_other().wait_send()
    for c_ in range(2):
        sent(bks.at[0:3, 0], bk_s.at[c_])
    sent(bka.at[0:3], ba_s.at[0])
    sent(dns.at[0:7], dn_s.at[0])
    for g in range(3):
        rs_other(g).wait_send()
        for c_ in range(2):
            sent(rss.at[g, c_, 0:7], rs_s.at[g, c_])
        sent(agu.at[g, 0, 0:7], gz_s.at[g])
        sent(agu.at[g, 0:3], gx_s.at[g])
    sent(agd.at[0, 0:7], gz_s.at[3])
    sent(agd.at[0:3], gx_s.at[3])


def spread(agu, agd, dn_out, up_out):
    def write(i, _):
        rows = pl.ds(pl.multiple_of(8 * i, 8), 8)
        for x_ in range(4):
            for c_ in range(2):
                lo = 256 * c_
                for h in range(2):
                    col = ((x_ * 2 + h) * 2 + c_) * 384
                    up_out[rows, col : col + 128] = agu[2, x_, i, :, lo + 128 * h : lo + 128 * (h + 1)].astype(F32)
                    up_out[rows, col + 128 : col + 384] = agu[h, x_, i, :, lo : lo + 256].astype(F32)
            dn_out[rows, 384 * x_ : 384 * (x_ + 1)] = agd[x_, i].astype(F32)
        return 0

    lax.fori_loop(0, 8, write, 0)


def on_device(frames, gain, w1, w2, down_map, up_map, lengths, cot):
    vmem = pl.BlockSpec(memory_space=pltpu.VMEM)
    dma = pltpu.SemaphoreType.DMA
    pieces = pl.pallas_call(
        kernel,
        out_shape=(
            jax.ShapeDtypeStruct((3, 4, 8, 8, 512), BF16),
            jax.ShapeDtypeStruct((4, 8, 8, 384), BF16),
        ),
        in_specs=[vmem, vmem, vmem, vmem, vmem, pl.BlockSpec(memory_space=pl.ANY),
                  pl.BlockSpec(memory_space=pltpu.SMEM), vmem],
        out_specs=(vmem, vmem),
        scratch_shapes=[
            pltpu.VMEM((2, 48, 128), BF16),
            pltpu.VMEM((2, 48, 256), BF16),
            pltpu.VMEM((2, 4, 8, 48, 256), BF16),
            pltpu.VMEM((2, 2, 4, 8, 48, 256), BF16),
            pltpu.VMEM((4, 2, ROWS, WIDE), BF16),
            pltpu.VMEM((2, 2, RANK, 384), BF16),
            pltpu.VMEM((4, 2, RANK, ROWS), F32),
            pltpu.VMEM((4, 2, RANK, ROWS), F32),
            pltpu.VMEM((4, RANK, ROWS), BF16),
            pltpu.VMEM((3, 2, 8, 8, 256), BF16),
            pltpu.VMEM((3, 8, 2, 8, 256), BF16),
            pltpu.VMEM((8, 8, 384), BF16),
            pltpu.VMEM((8, 8, 384), BF16),
            dma((4,)), dma((4,)), dma((1,)), dma((1,)), dma((1,)), dma((6,)), dma((1,)), dma((1,)), dma((4,)), dma((2,)),
            dma((2,)), dma((2, 2, 8)), dma((2,)), dma((2, 2, 8)),
            dma((3,)), dma((3, 16)), dma((2,)), dma((2,)),
            dma((3,)), dma((3,)), dma((1,)), dma((1,)), dma((3, 3)), dma((3, 3)),
            dma((1,)), dma((1,)), dma((4,)), dma((4, 3)), dma((4,)), dma((4, 6)),
        ],
        compiler_params=pltpu.CompilerParams(
            collective_id=0, has_side_effects=True, vmem_limit_bytes=56 * 1024 * 1024
        ),
    )(frames, gain, w1, w2.T, down_map[0].T, up_map, lengths, cot)
    dn, up = pl.pallas_call(
        spread,
        out_shape=(
            jax.ShapeDtypeStruct((RANK, D), F32),
            jax.ShapeDtypeStruct((RANK, 6144), F32),
        ),
        in_specs=[vmem, vmem],
        out_specs=(vmem, vmem),
    )(*pieces)
    return dn.T[None], up[None]


def solution(mesh):
    in_specs = (
        P("member", "fsdp", None),
        P(),
        P("fsdp", "member"),
        P("member", "fsdp"),
        P("member", None, None),
        P("member", None, None),
        P("member", "fsdp"),
        P("member", "fsdp", None),
    )
    out_specs = (P("member", None, None), P("member", None, None))
    return jax.shard_map(
        on_device, mesh=mesh, in_specs=in_specs, out_specs=out_specs, check_vma=False
    )
```

```python
import jax
import jax.numpy as jnp
from jax import lax
from jax.experimental import pallas as pl
from jax.experimental.pallas import tpu as pltpu
from jax.sharding import PartitionSpec as P

MESH = pl.DeviceIdType.MESH
ROWS = 128
D = 1536
RANK = 64
LOW = D
COT = D + 128
WIDE = 2 * D + 128
F32 = jnp.float32
BF16 = jnp.bfloat16


def dot(a, b, dims=((1,), (0,))):
    return lax.dot_general(a, b, (dims, ((), ())), preferred_element_type=F32)


def kernel(
    frames_, gain, w1, w2t, down_map_, up_map, lengths, cot_,
    ou, od,
    agu, agd, ws_a, ws_b, wa, wb, tok, ub, bks, bkr, bka, rss, rsr, dns, dnr,
    ta_s, ta_r, tb_s, tb_r, tk_s, tk_r, td_s, td_r, u_s, u_r,
    az_s, az_r, bz_s, bz_r, by_s, by_r, bo_s, bo_r,
    bk_s, bk_r, ba_s, ba_r, rs_s, rs_r, dn_s, dn_r, gz_s, gz_r, gx_s, gx_r, o_s, frames, cot, down_map, i_s,
):
    fi = lax.axis_index("fsdp")
    mi = lax.axis_index("member")
    x, zl = fi // 8, fi % 8
    y, zh, c = mi // 4, (mi // 2) % 2, mi % 2
    z = zh * 8 + zl

    def dev(x_, y_, z_, c_):
        return (x_ * 8 + z_ % 8, y_ * 4 + (z_ // 8) * 2 + c_)

    xr, xl, xo = (x + 1) % 4, (x + 3) % 4, (x + 2) % 4
    yr, yl, yo = (y + 1) % 4, (y + 3) % 4, (y + 2) % 4
    right, left = dev(xr, y, z, c), dev(xl, y, z, c)
    up, dn = dev(x, yr, z, c), dev(x, yl, z, c)
    fore, aft = dev(x, y, (z + 1) % 16, c), dev(x, y, (z + 15) % 16, c)
    twin = dev(x, y, z, 1 - c)
    flip = dev(y, x, z, c)

    def zdev(d, c_):
        return dev(x, y, zh * 8 + (zl + d) % 8, c_)

    def rcopy(src, dst, ss, rs, to):
        return pltpu.make_async_remote_copy(
            src_ref=src, dst_ref=dst, send_sem=ss, recv_sem=rs, device_id=to, device_id_type=MESH
        )

    def sent(ref, sem):
        rcopy(ref, ref, sem, sem, right).wait_send()

    def got(ref, sem):
        rcopy(ref, ref, sem, sem, right).wait_recv()

    fetch = [
        pltpu.make_async_copy(frames_.at[:, 0:ROWS], frames, i_s.at[0]),
        pltpu.make_async_copy(cot_.at[:, 0:ROWS], cot, i_s.at[1]),
        pltpu.make_async_copy(down_map_, down_map, i_s.at[2]),
    ]
    for cp in fetch:
        cp.start()

    barrier = pltpu.get_barrier_semaphore()
    peers = [up, dn, dev(x, yo, z, c), fore, aft, twin]
    for d in range(1, 4):
        for c_ in range(2):
            peers.append(dev((x + d) % 4, y, z, c_))
    for d in range(1, 8):
        for c_ in range(2):
            peers.append(zdev(d, c_))
    for peer in peers:
        pl.semaphore_signal(barrier, inc=1, device_id=peer, device_id_type=MESH)

    @pl.when(x != y)
    def _():
        pl.semaphore_signal(barrier, inc=1, device_id=flip, device_id_type=MESH)

    ws_a[0] = w1[:, 0:128]
    ws_b[0] = w1[:, 128:384]
    ws_a[1] = w2t[:, 0:128]
    ws_b[1] = w2t[:, 128:384]

    pl.semaphore_wait(barrier, len(peers) + jnp.where(x != y, 1, 0))

    def lanes(zh_):
        return pl.ds(pl.multiple_of(zh_ * 128, 128), 128)

    def ta_slot(y_):
        return wa.at[:, y_, zl, :, lanes(zh)]

    def ta_copy():
        return rcopy(ws_a, ta_slot(x), ta_s.at[0], ta_r.at[0], flip)

    def ta_pass(e):
        return rcopy(ta_slot(y), ta_slot(y), ta_s.at[1], ta_r.at[e], dev(x, (y + e) % 4, z, c))

    def ta_wait(e):
        got(ta_slot((y + 4 - e) % 4), ta_r.at[e])

    def tb_copy():
        return rcopy(ws_b, wb.at[zh, :, x, zl], tb_s.at[0], tb_r.at[0], flip)

    @pl.when(x != y)
    def _():
        tb_copy().start()
        ta_copy().start()

    @pl.when(x == y)
    def _():
        for w in range(2):
            wa[w, y, zl, :, lanes(zh)] = ws_a[w]
            wb[zh, w, y, zl] = ws_b[w]

    for cp in fetch:
        cp.wait()
    v = frames[0, 0:ROWS, :].astype(F32)
    mean = jnp.mean(v, axis=1, keepdims=True)
    var = jnp.mean((v - mean) ** 2, axis=1, keepdims=True)
    normed = (gain[...][None, :] * (v - mean) / jnp.sqrt(var + 1e-05)).astype(BF16)
    low = dot(normed, down_map[...], ((1,), (1,))).astype(BF16)
    keep = lax.broadcasted_iota(jnp.int32, (ROWS, D), 0) < lengths[0, 0]
    masked = jnp.where(keep, cot[0, 0:ROWS, :].astype(F32), 0.0).astype(BF16)
    tok[x, c, :, 0:D] = normed
    tok[x, c, :, LOW : LOW + 128] = jnp.concatenate([low, jnp.zeros_like(low)], axis=1)
    tok[x, c, :, COT:WIDE] = masked

    def half(x_, h):
        return tok.at[x_, c, pl.ds(64 * h, 64), :]

    def halfo(x_, h):
        return tok.at[x_, 1 - c, pl.ds(64 * h, 64), :]

    def t_copy(i):
        x_, h, to = [
            (x, 0, right), (x, 1, right), (x, 1, left), (x, 0, left), (xl, 0, right), (xr, 1, left)
        ][i]
        return rcopy(half(x_, h), half(x_, h), tk_s.at[0], tk_r.at[i], to)

    def t_wait(i):
        x_, h = [(xl, 0), (xl, 1), (xr, 1), (xr, 0), (xo, 0), (xo, 1)][i]
        got(half(x_, h), tk_r.at[i])

    def d_copy(r, h):
        x_ = [x, xl, xr, xo][r]
        return rcopy(half(x_, h), half(x_, h), td_s.at[0], td_r.at[0], twin)

    for i in (0, 2, 1, 3):
        t_copy(i).start()

    def a_str(s, e):
        z_ = (z + s + 16) % 16
        return wa.at[:, (y + 4 - e) % 4, z_ % 8, :, lanes(z_ // 8)]

    def b_str(s, w):
        return b_half(s, y, w)

    def b_blk(s, y_):
        z_ = (z + s + 16) % 16
        return wb.at[z_ // 8, :, y_, z_ % 8]

    def b_half(s, y_, w):
        z_ = (z + s + 16) % 16
        return wb.at[z_ // 8, w, y_, z_ % 8]

    streams = [(b_str, bz_s, bz_r), (a_str, az_s, az_r)]

    def z_copy(i, w, route, k):
        make, ss, rs = streams[i]
        blk = make((-(k - 1)) if route == 0 else (k - 1), w)
        return rcopy(blk, blk, ss.at[route], rs.at[route, w, k - 1], fore if route == 0 else aft)

    def z_wait(i, w, route, k):
        make, ss, rs = streams[i]
        blk = make(-k if route == 0 else k, w)
        got(blk, rs.at[route, w, k - 1])

    def by_copy(s, j, way):
        return rcopy(b_blk(s, y), b_blk(s, y), by_s.at[way], by_r.at[way, j], up if way == 0 else dn)

    def by_wait(s, j, way):
        y_ = yl if way == 0 else yr
        got(b_blk(s, y_), by_r.at[way, j])

    def by_last(way):
        blk = b_blk(8, y)
        return rcopy(blk, blk, by_s.at[way], by_r.at[way, 15], [up, dn, dev(x, yo, z, c)][way])

    def by_last_wait(way):
        blk = b_blk(8, [yl, yr, yo][way])
        got(blk, by_r.at[way, 15])

    def bo_copy(s, way):
        y_ = yl if way == 0 else yr
        return rcopy(
            b_half(s, y_, way), b_half(s, y_, way), bo_s.at[way], bo_r.at[way], up if way == 0 else dn
        )

    @pl.when(x != y)
    def _():
        blk = wb.at[zh, :, y, zl]
        rcopy(blk, blk, tb_s.at[0], tb_r.at[0], flip).wait_recv()

    for w in range(2):
        for route in range(2):
            z_copy(0, w, route, 1).start()
    @pl.when(x != y)
    def _():
        ta_wait(0)

    for e_ in range(1, 4):
        ta_pass(e_).start()
    for way in range(2):
        by_copy(0, 0, way).start()
    for e in range(4):
        if e > 0:
            ta_wait(e)
        for route in range(2):
            z_copy(1, e, route, 1).start()

    for h in range(2):
        d_copy(0, h).start()

    def u_cols(zh_, c_):
        return up_map.at[0, :, pl.ds(pl.multiple_of(((x * 2 + zh_) * 2 + c_) * 384, 128), 384)]

    def u_local(zh_):
        return pltpu.make_async_copy(u_cols(zh_, c), ub.at[c, zh_], u_s.at[2 + zh_])

    def u_copy(zh_):
        return rcopy(u_cols(zh_, 1 - c), ub.at[c, zh_], u_s.at[zh_], u_r.at[zh_], twin)

    for zh_ in range(2):
        u_local(zh_).start()
        u_copy(zh_).start()

    def y_stage(s, j):
        for way in range(2):
            by_wait(s, j, way)
            bo_copy(s, way).start()

    def step(k, _):
        for w in range(2):
            for route in range(2):
                z_wait(0, w, route, k)
                z_copy(0, w, route, k + 1).start()
        for route in range(2):
            for way in range(2):
                by_copy(-k if route == 0 else k, 2 * k - 1 + route, way).start()
        for e in range(4):
            for route in range(2):
                z_wait(1, e, route, k)
                z_copy(1, e, route, k + 1).start()
        for route in range(2):
            s = -(k - 1) if route == 0 else (k - 1)

            @pl.when((k > 1) | (route == 0))
            def _():
                y_stage(s, jnp.where(k == 1, 0, 2 * k - 3 + route))
        return 0

    lax.fori_loop(1, 4, step, 0)
    t_wait(0)
    t_copy(4).start()
    d_copy(1, 0).start()
    t_wait(2)
    t_copy(5).start()
    d_copy(2, 1).start()
    lax.fori_loop(4, 7, step, 0)
    t_wait(1)
    d_copy(1, 1).start()
    t_wait(3)
    d_copy(2, 0).start()
    for w in range(2):
        for route in range(2):
            z_wait(0, w, route, 7)
            if route == w:
                z_copy(0, w, route, 8).start()
    for route in range(2):
        for way in range(2):
            by_copy(-7 if route == 0 else 7, 13 + route, way).start()
    for e in range(4):
        for route in range(2):
            z_wait(1, e, route, 7)
            if route == e // 2:
                z_copy(1, e, route, 8).start()
    y_stage(-6, 11)
    y_stage(6, 12)
    for w in range(2):
        z_wait(0, w, w, 8)
    for way in range(3):
        by_last(way).start()
    y_stage(-7, 13)
    y_stage(7, 14)
    for i in (4, 5):
        t_wait(i)
        d_copy(3, i - 4).start()
    for e in range(4):
        z_wait(1, e, e // 2, 8)

    got(tok.at[:, 0], td_r.at[0])
    for zh_ in range(2):
        u_local(zh_).wait()
        rcopy(ub.at[1 - c, zh_], ub.at[1 - c, zh_], u_s.at[zh_], u_r.at[zh_], twin).wait_recv()

    def third(g):
        def member(m, _):
            lo = tok[:, m, :, LOW : LOW + 128].reshape(4 * ROWS, 128)
            if g < 2:
                wi, wo = wb[g, 0].reshape(D, 256), wb[g, 1].reshape(D, 256)
                u = ub[m, g, :, 128:384]
            else:
                wi, wo = wa[0].reshape(D, 256), wa[1].reshape(D, 256)
                u = jnp.concatenate([ub[m, 0, :, 0:128], ub[m, 1, :, 0:128]], axis=1)
            pre = dot(tok[:, m, :, 0:D].reshape(4 * ROWS, D), wi) + dot(lo[:, 0:RANK], u)
            dhid = 0.5 * dot(tok[:, m, :, COT:WIDE].reshape(4 * ROWS, D), wo)
            sig = jax.nn.sigmoid(pre)
            dpre = (dhid * sig * (1.0 + pre * (1.0 - sig))).astype(BF16)
            part = dot(lo, dpre, ((0,), (0,)))
            for r in range(8):
                rss[g, m, r] = part[8 * r : 8 * r + 8].astype(BF16)
            for x_ in range(4):
                bp = dot(u, dpre[ROWS * x_ : ROWS * (x_ + 1)], ((1,), (1,)))
                if g == 2:
                    bks[x_, m] = bp
                else:
                    bks[x_, m] += bp
            return 0

        lax.fori_loop(0, 2, member, 0)

    def rs_copy(g, d, c_):
        return rcopy(
            rss.at[g, c_, (zl + d) % 8], rsr.at[g, zl, c], rs_s.at[g, c_], rs_r.at[g, c], zdev(d, c_)
        )

    def rs_other(g):
        return rcopy(rss.at[g, 1 - c, zl], rsr.at[g, zl, c], rs_s.at[g, 2], rs_r.at[g, 2], twin)

    def rs_start(g):
        for d in (4, 3, 5, 2, 6, 1, 7):
            for c_ in range(2):
                rs_copy(g, d, c_).start()
        rs_other(g).start()
        rsr[g, zl, c] = rss[g, c, zl]

    def rs_sum(g):
        got(rsr.at[g, zl, 1 - c], rs_r.at[g, 2])
        for c_ in range(2):
            got(rsr.at[g, 0:7, c_], rs_r.at[g, c_])
        for c_ in range(2):
            total = rsr[g, 0, c_].astype(F32)
            for i in range(1, 8):
                total = total + rsr[g, i, c_].astype(F32)
            agu[g, x, zl, :, 256 * c_ : 256 * (c_ + 1)] = total.astype(BF16)

    def bk_copy(d, c_):
        x_ = (x + d) % 4
        return rcopy(bks.at[x_, c_], bkr.at[x, c], bk_s.at[c_], bk_r.at[c], dev(x_, y, z, c_))

    def bk_other():
        return rcopy(bks.at[x, 1 - c], bkr.at[x, c], bk_s.at[2], bk_r.at[2], twin)

    def ba_copy(d):
        return rcopy(bka.at[x], bka.at[x], ba_s.at[0], ba_r.at[0], dev((x + d) % 4, y, z, c))

    def dn_copy(d):
        return rcopy(dns.at[(zl + d) % 8], dnr.at[zl], dn_s.at[0], dn_r.at[0], zdev(d, c))

    z4, q4 = (zl // 4) * 4, zl % 4
    far = (zl + 4) % 8

    def piece(g, zl_):
        return agd.at[x, zl_] if g == 3 else agu.at[g, x, zl_]

    def near(j):
        return dev(x, y, zh * 8 + z4 + (q4 + j) % 4, c)

    def gz_copy(g, j):
        if j == 0:
            return rcopy(piece(g, zl), piece(g, zl), gz_s.at[g], gz_r.at[g, 0], dev(x, y, zh * 8 + far, c))
        src = zl if j < 4 else far
        return rcopy(piece(g, src), piece(g, src), gz_s.at[g], gz_r.at[g, 1 if j < 4 else 2], near((j - 1) % 3 + 1))

    def gz_wait(g, i):
        got(agu.at[g, 0, 0:1] if i == 0 else agu.at[g, 0, 0:3], gz_r.at[g, i])

    def gz_all(g):
        for d in (4, 3, 5, 2, 6, 1, 7):
            rcopy(piece(g, zl), piece(g, zl), gz_s.at[g], gz_r.at[g, 0], zdev(d, c)).start()

    def gz_all_wait(g):
        got(agd.at[0, 0:7] if g == 3 else agu.at[g, 0, 0:7], gz_r.at[g, 0])

    def g_half(g, x_, h):
        return agu.at[g, x_, pl.ds(z4 if h == 0 else 4 - z4, 4)]

    def gx_copy(g, i):
        x_, h, to = [
            (x, 0, right), (x, 1, right), (x, 1, left), (x, 0, left), (xl, 0, right), (xr, 1, left)
        ][i]
        return rcopy(g_half(g, x_, h), g_half(g, x_, h), gx_s.at[g], gx_r.at[g, i], to)

    def gx_wait(g, i):
        x_, h = [(xl, 0), (xl, 1), (xr, 1), (xr, 0), (xo, 0), (xo, 1)][i]
        got(g_half(g, x_, h), gx_r.at[g, i])

    def gd_copy(d):
        return rcopy(agd.at[x], agd.at[x], gx_s.at[3], gx_r.at[3, 0], dev((x + d) % 4, y, z, c))

    def gz_own(g):
        for j in range(4):
            gz_copy(g, j).start()

    def gz_pass(g):
        gz_wait(g, 0)
        for j in range(4, 7):
            gz_copy(g, j).start()

    def gx_first(g):
        gz_wait(g, 1)
        gx_copy(g, 0).start()
        gx_copy(g, 3).start()

    def gx_second(g):
        gz_wait(g, 2)
        gx_copy(g, 2).start()
        gx_copy(g, 1).start()

    def gx_pass(g):
        gx_wait(g, 0)
        gx_copy(g, 4).start()
        gx_wait(g, 2)
        gx_copy(g, 5).start()

    third(2)
    rs_start(2)
    for way in range(3):
        by_last_wait(way)
    for way in range(2):
        got(wb.at[0, 0, 0:3, 0:5], bo_r.at[way])
    third(0)
    rs_start(0)
    third(1)
    for d in range(1, 4):
        for c_ in range(2):
            bk_copy(d, c_).start()
    bk_other().start()
    rs_start(1)
    bkr[x, c] = bks[x, c]

    got(bkr.at[x, 1 - c], bk_r.at[2])
    for c_ in range(2):
        got(bkr.at[0:3, c_], bk_r.at[c_])
    total = bkr[0, 0]
    for i in range(1, 8):
        total = total + bkr[i // 2, i % 2]
    bka[x] = total.astype(BF16)
    for d in range(1, 4):
        ba_copy(d).start()

    rs_sum(2)
    gz_own(2)
    rs_sum(0)
    gz_own(0)

    got(bka.at[0:3], ba_r.at[0])
    quarter = pl.ds(pl.multiple_of(x * 384, 128), 384)
    part = dot(bka[0], tok[0, c, :, quarter])
    for x_ in range(1, 4):
        part = part + dot(bka[x_], tok[x_, c, :, quarter])
    for r in range(8):
        dns[r] = part[8 * r : 8 * r + 8].astype(BF16)
    for d in range(1, 8):
        dn_copy(d).start()
    dnr[zl] = dns[zl]

    rs_sum(1)
    gz_own(1)
    gz_pass(2)
    gx_first(2)
    gz_pass(0)
    gx_first(0)
    gx_second(2)
    got(dnr.at[0:7], dn_r.at[0])
    total = dnr[0].astype(F32)
    for i in range(1, 8):
        total = total + dnr[i].astype(F32)
    agd[x, zl] = total.astype(BF16)
    gz_all(3)
    gz_pass(1)
    gx_second(0)
    gx_pass(2)
    gx_first(1)
    gx_second(1)
    gx_pass(0)
    gz_all_wait(3)
    for d in range(1, 4):
        gd_copy(d).start()
    gx_pass(1)
    outs = [pltpu.make_async_copy(agu.at[g], ou.at[g], o_s.at[g]) for g in range(3)]
    outs.append(pltpu.make_async_copy(agd, od, o_s.at[3]))
    for g in (2, 0, 1):
        for i in (1, 3, 4, 5):
            gx_wait(g, i)
        outs[g].start()
    got(agd.at[0:3], gx_r.at[3, 0])
    outs[3].start()

    @pl.when(x != y)
    def _():
        tb_copy().wait_send()
        ta_copy().wait_send()

    sent(wa.at[:, 0:3, 0, :, 0:128], ta_s.at[1])
    sent(tok.at[0:3, 0], tk_s.at[0])
    sent(tok.at[:, 0], td_s.at[0])
    for zh_ in range(2):
        u_copy(zh_).wait_send()
    for route in range(2):
        sent(wa.at[0:2, 0:3, 0:5], az_s.at[route])
        sent(wb.at[0, 0, 0:3, 0:5], bz_s.at[route])
        sent(wb.at[0, 0], by_s.at[route])
        sent(wb.at[0, 0, 0:3, 0:5], bo_s.at[route])
    sent(wb.at[0, 0, 0, 0:2], by_s.at[2])
    bk_other().wait_send()
    for c_ in range(2):
        sent(bks.at[0:3, 0], bk_s.at[c_])
    sent(bka.at[0:3], ba_s.at[0])
    sent(dns.at[0:7], dn_s.at[0])
    for g in range(3):
        rs_other(g).wait_send()
        for c_ in range(2):
            sent(rss.at[g, c_, 0:7], rs_s.at[g, c_])
        sent(agu.at[g, 0, 0:7], gz_s.at[g])
        sent(agu.at[g, 0:3], gx_s.at[g])
    sent(agd.at[0, 0:7], gz_s.at[3])
    sent(agd.at[0:3], gx_s.at[3])
    for out in outs:
        out.wait()


def spread(agu, agd, dn_out, up_out):
    def write(i, _):
        rows = pl.ds(pl.multiple_of(8 * i, 8), 8)
        for x_ in range(4):
            for c_ in range(2):
                lo = 256 * c_
                for h in range(2):
                    col = ((x_ * 2 + h) * 2 + c_) * 384
                    up_out[rows, col : col + 128] = agu[2, x_, i, :, lo + 128 * h : lo + 128 * (h + 1)].astype(F32)
                    up_out[rows, col + 128 : col + 384] = agu[h, x_, i, :, lo : lo + 256].astype(F32)
            dn_out[rows, 384 * x_ : 384 * (x_ + 1)] = agd[x_, i].astype(F32)
        return 0

    lax.fori_loop(0, 8, write, 0)


def on_device(frames, gain, w1, w2, down_map, up_map, lengths, cot):
    vmem = pl.BlockSpec(memory_space=pltpu.VMEM)
    hbm = pl.BlockSpec(memory_space=pl.ANY)
    dma = pltpu.SemaphoreType.DMA
    pieces = pl.pallas_call(
        kernel,
        out_shape=(
            jax.ShapeDtypeStruct((3, 4, 8, 8, 512), BF16),
            jax.ShapeDtypeStruct((4, 8, 8, 384), BF16),
        ),
        in_specs=[hbm, vmem, vmem, vmem, hbm, hbm, pl.BlockSpec(memory_space=pltpu.SMEM), hbm],
        out_specs=(pl.BlockSpec(memory_space=pl.ANY), pl.BlockSpec(memory_space=pl.ANY)),
        scratch_shapes=[
            pltpu.VMEM((3, 4, 8, 8, 512), BF16),
            pltpu.VMEM((4, 8, 8, 384), BF16),
            pltpu.VMEM((2, 48, 128), BF16),
            pltpu.VMEM((2, 48, 256), BF16),
            pltpu.VMEM((2, 4, 8, 48, 256), BF16),
            pltpu.VMEM((2, 2, 4, 8, 48, 256), BF16),
            pltpu.VMEM((4, 2, ROWS, WIDE), BF16),
            pltpu.VMEM((2, 2, RANK, 384), BF16),
            pltpu.VMEM((4, 2, RANK, ROWS), F32),
            pltpu.VMEM((4, 2, RANK, ROWS), F32),
            pltpu.VMEM((4, RANK, ROWS), BF16),
            pltpu.VMEM((3, 2, 8, 8, 256), BF16),
            pltpu.VMEM((3, 8, 2, 8, 256), BF16),
            pltpu.VMEM((8, 8, 384), BF16),
            pltpu.VMEM((8, 8, 384), BF16),
            dma((4,)), dma((4,)), dma((1,)), dma((1,)), dma((1,)), dma((6,)), dma((1,)), dma((1,)), dma((4,)), dma((2,)),
            dma((2,)), dma((2, 4, 8)), dma((2,)), dma((2, 2, 8)),
            dma((3,)), dma((3, 16)), dma((2,)), dma((2,)),
            dma((3,)), dma((3,)), dma((1,)), dma((1,)), dma((3, 3)), dma((3, 3)),
            dma((1,)), dma((1,)), dma((4,)), dma((4, 3)), dma((4,)), dma((4, 6)), dma((4,)),
            pltpu.VMEM((1, ROWS, D), BF16),
            pltpu.VMEM((1, ROWS, D), BF16),
            pltpu.VMEM((RANK, D), BF16),
            dma((3,)),
        ],
        compiler_params=pltpu.CompilerParams(
            collective_id=0, has_side_effects=True, vmem_limit_bytes=56 * 1024 * 1024
        ),
    )(frames, gain, w1, w2.T, down_map[0].T, up_map, lengths, cot)
    dn, up = pl.pallas_call(
        spread,
        out_shape=(
            jax.ShapeDtypeStruct((RANK, D), F32),
            jax.ShapeDtypeStruct((RANK, 6144), F32),
        ),
        in_specs=[vmem, vmem],
        out_specs=(vmem, vmem),
    )(*pieces)
    return dn.T[None], up[None]


def solution(mesh):
    in_specs = (
        P("member", "fsdp", None),
        P(),
        P("fsdp", "member"),
        P("member", "fsdp"),
        P("member", None, None),
        P("member", None, None),
        P("member", "fsdp"),
        P("member", "fsdp", None),
    )
    out_specs = (P("member", None, None), P("member", None, None))
    return jax.shard_map(
        on_device, mesh=mesh, in_specs=in_specs, out_specs=out_specs, check_vma=False
    )
```

```python
import jax
import jax.numpy as jnp
from jax import lax
from jax.experimental import pallas as pl
from jax.experimental.pallas import tpu as pltpu
from jax.sharding import PartitionSpec as P

MESH = pl.DeviceIdType.MESH
ROWS = 128
D = 1536
RANK = 64
LOW = D
COT = D + 128
WIDE = 2 * D + 128
F32 = jnp.float32
BF16 = jnp.bfloat16


def dot(a, b, dims=((1,), (0,))):
    return lax.dot_general(a, b, (dims, ((), ())), preferred_element_type=F32)


def kernel(
    frames_, gain, w1, w2t, down_map_, up_map, lengths, cot_,
    ou, od,
    agu, agd, ws_a, ws_b, wa, wb, tok, ub, bks, bkr, bka, rss, rsr, dns, dnr,
    ta_s, ta_r, tb_s, tb_r, tk_s, tk_r, td_s, td_r, u_s, u_r,
    az_s, az_r, bz_s, bz_r, by_s, by_r, bo_s, bo_r,
    bk_s, bk_r, ba_s, ba_r, rs_s, rs_r, dn_s, dn_r, gz_s, gz_r, gx_s, gx_r, o_s, frames, cot, down_map, i_s,
):
    fi = lax.axis_index("fsdp")
    mi = lax.axis_index("member")
    x, zl = fi // 8, fi % 8
    y, zh, c = mi // 4, (mi // 2) % 2, mi % 2
    z = zh * 8 + zl

    def dev(x_, y_, z_, c_):
        return (x_ * 8 + z_ % 8, y_ * 4 + (z_ // 8) * 2 + c_)

    xr, xl, xo = (x + 1) % 4, (x + 3) % 4, (x + 2) % 4
    yr, yl, yo = (y + 1) % 4, (y + 3) % 4, (y + 2) % 4
    right, left = dev(xr, y, z, c), dev(xl, y, z, c)
    up, dn = dev(x, yr, z, c), dev(x, yl, z, c)
    fore, aft = dev(x, y, (z + 1) % 16, c), dev(x, y, (z + 15) % 16, c)
    twin = dev(x, y, z, 1 - c)
    flip = dev(y, x, z, c)

    def zdev(d, c_):
        return dev(x, y, zh * 8 + (zl + d) % 8, c_)

    def rcopy(src, dst, ss, rs, to):
        return pltpu.make_async_remote_copy(
            src_ref=src, dst_ref=dst, send_sem=ss, recv_sem=rs, device_id=to, device_id_type=MESH
        )

    def sent(ref, sem):
        rcopy(ref, ref, sem, sem, right).wait_send()

    def got(ref, sem):
        rcopy(ref, ref, sem, sem, right).wait_recv()

    fetch = [
        pltpu.make_async_copy(frames_.at[:, 0:ROWS], frames, i_s.at[0]),
        pltpu.make_async_copy(cot_.at[:, 0:ROWS], cot, i_s.at[1]),
        pltpu.make_async_copy(down_map_, down_map, i_s.at[2]),
    ]
    for cp in fetch:
        cp.start()

    barrier = pltpu.get_barrier_semaphore()
    peers = [up, dn, dev(x, yo, z, c), fore, aft, twin]
    for d in range(1, 4):
        for c_ in range(2):
            peers.append(dev((x + d) % 4, y, z, c_))
    for d in range(1, 8):
        for c_ in range(2):
            peers.append(zdev(d, c_))
    for peer in peers:
        pl.semaphore_signal(barrier, inc=1, device_id=peer, device_id_type=MESH)

    @pl.when(x != y)
    def _():
        pl.semaphore_signal(barrier, inc=1, device_id=flip, device_id_type=MESH)

    ws_a[0] = w1[:, 0:128]
    ws_b[0] = w1[:, 128:384]
    ws_a[1] = w2t[:, 0:128]
    ws_b[1] = w2t[:, 128:384]

    pl.semaphore_wait(barrier, len(peers) + jnp.where(x != y, 1, 0))

    def lanes(zh_):
        return pl.ds(pl.multiple_of(zh_ * 128, 128), 128)

    def ta_slot(y_):
        return wa.at[:, y_, zl, :, lanes(zh)]

    def ta_copy():
        return rcopy(ws_a, ta_slot(x), ta_s.at[0], ta_r.at[0], flip)

    def ta_pass(e):
        return rcopy(ta_slot(y), ta_slot(y), ta_s.at[1], ta_r.at[e], dev(x, (y + e) % 4, z, c))

    def ta_wait(e):
        got(ta_slot((y + 4 - e) % 4), ta_r.at[e])

    def tb_copy():
        return rcopy(ws_b, wb.at[zh, :, x, zl], tb_s.at[0], tb_r.at[0], flip)

    @pl.when(x != y)
    def _():
        tb_copy().start()
        ta_copy().start()

    @pl.when(x == y)
    def _():
        for w in range(2):
            wa[w, y, zl, :, lanes(zh)] = ws_a[w]
            wb[zh, w, y, zl] = ws_b[w]

    for cp in fetch:
        cp.wait()
    v = frames[0, 0:ROWS, :].astype(F32)
    mean = jnp.mean(v, axis=1, keepdims=True)
    var = jnp.mean((v - mean) ** 2, axis=1, keepdims=True)
    normed = (gain[...][None, :] * (v - mean) / jnp.sqrt(var + 1e-05)).astype(BF16)
    low = dot(normed, down_map[...], ((1,), (1,))).astype(BF16)
    keep = lax.broadcasted_iota(jnp.int32, (ROWS, D), 0) < lengths[0, 0]
    masked = jnp.where(keep, cot[0, 0:ROWS, :].astype(F32), 0.0).astype(BF16)
    tok[x, c, :, 0:D] = normed
    tok[x, c, :, LOW : LOW + 128] = jnp.concatenate([low, jnp.zeros_like(low)], axis=1)
    tok[x, c, :, COT:WIDE] = masked

    def half(x_, h):
        return tok.at[x_, c, pl.ds(64 * h, 64), :]

    def halfo(x_, h):
        return tok.at[x_, 1 - c, pl.ds(64 * h, 64), :]

    def t_copy(i):
        x_, h, to = [
            (x, 0, right), (x, 1, right), (x, 1, left), (x, 0, left), (xl, 0, right), (xr, 1, left)
        ][i]
        return rcopy(half(x_, h), half(x_, h), tk_s.at[0], tk_r.at[i], to)

    def t_wait(i):
        x_, h = [(xl, 0), (xl, 1), (xr, 1), (xr, 0), (xo, 0), (xo, 1)][i]
        got(half(x_, h), tk_r.at[i])

    def d_copy(r, h):
        x_ = [x, xl, xr, xo][r]
        return rcopy(half(x_, h), half(x_, h), td_s.at[0], td_r.at[0], twin)

    for i in (0, 2, 1, 3):
        t_copy(i).start()

    def a_str(s, e):
        z_ = (z + s + 16) % 16
        return wa.at[:, (y + 4 - e) % 4, z_ % 8, :, lanes(z_ // 8)]

    def b_str(s, w):
        return b_half(s, y, w)

    def b_blk(s, y_):
        z_ = (z + s + 16) % 16
        return wb.at[z_ // 8, :, y_, z_ % 8]

    def b_half(s, y_, w):
        z_ = (z + s + 16) % 16
        return wb.at[z_ // 8, w, y_, z_ % 8]

    streams = [(b_str, bz_s, bz_r), (a_str, az_s, az_r)]

    def z_copy(i, w, route, k):
        make, ss, rs = streams[i]
        blk = make((-(k - 1)) if route == 0 else (k - 1), w)
        return rcopy(blk, blk, ss.at[route], rs.at[route, w, k - 1], fore if route == 0 else aft)

    def z_wait(i, w, route, k):
        make, ss, rs = streams[i]
        blk = make(-k if route == 0 else k, w)
        got(blk, rs.at[route, w, k - 1])

    def by_copy(s, j, way):
        return rcopy(b_blk(s, y), b_blk(s, y), by_s.at[way], by_r.at[way, j], up if way == 0 else dn)

    def by_wait(s, j, way):
        y_ = yl if way == 0 else yr
        got(b_blk(s, y_), by_r.at[way, j])

    def by_last(way):
        blk = b_blk(8, y)
        return rcopy(blk, blk, by_s.at[way], by_r.at[way, 15], [up, dn, dev(x, yo, z, c)][way])

    def by_last_wait(way):
        blk = b_blk(8, [yl, yr, yo][way])
        got(blk, by_r.at[way, 15])

    def bo_copy(s, way):
        y_ = yl if way == 0 else yr
        return rcopy(
            b_half(s, y_, way), b_half(s, y_, way), bo_s.at[way], bo_r.at[way], up if way == 0 else dn
        )

    @pl.when(x != y)
    def _():
        blk = wb.at[zh, :, y, zl]
        rcopy(blk, blk, tb_s.at[0], tb_r.at[0], flip).wait_recv()

    for w in range(2):
        for route in range(2):
            z_copy(0, w, route, 1).start()
    @pl.when(x != y)
    def _():
        ta_wait(0)

    for e_ in range(1, 4):
        ta_pass(e_).start()
    for way in range(2):
        by_copy(0, 0, way).start()
    for e in range(4):
        if e > 0:
            ta_wait(e)
        for route in range(2):
            z_copy(1, e, route, 1).start()

    for h in range(2):
        d_copy(0, h).start()

    def u_cols(zh_, c_):
        return up_map.at[0, :, pl.ds(pl.multiple_of(((x * 2 + zh_) * 2 + c_) * 384, 128), 384)]

    def u_local(zh_):
        return pltpu.make_async_copy(u_cols(zh_, c), ub.at[c, zh_], u_s.at[2 + zh_])

    def u_copy(zh_):
        return rcopy(u_cols(zh_, 1 - c), ub.at[c, zh_], u_s.at[zh_], u_r.at[zh_], twin)

    for zh_ in range(2):
        u_local(zh_).start()
        u_copy(zh_).start()

    def y_stage(s, j):
        for way in range(2):
            by_wait(s, j, way)
            bo_copy(s, way).start()

    def step(k, _):
        for w in range(2):
            for route in range(2):
                z_wait(0, w, route, k)
                z_copy(0, w, route, k + 1).start()
        for route in range(2):
            for way in range(2):
                by_copy(-k if route == 0 else k, 2 * k - 1 + route, way).start()
        for e in range(4):
            for route in range(2):
                z_wait(1, e, route, k)
                z_copy(1, e, route, k + 1).start()
        for route in range(2):
            s = -(k - 1) if route == 0 else (k - 1)

            @pl.when((k > 1) | (route == 0))
            def _():
                y_stage(s, jnp.where(k == 1, 0, 2 * k - 3 + route))
        return 0

    lax.fori_loop(1, 4, step, 0)
    t_wait(0)
    t_copy(4).start()
    d_copy(1, 0).start()
    t_wait(2)
    t_copy(5).start()
    d_copy(2, 1).start()
    lax.fori_loop(4, 7, step, 0)
    t_wait(1)
    d_copy(1, 1).start()
    t_wait(3)
    d_copy(2, 0).start()
    for w in range(2):
        for route in range(2):
            z_wait(0, w, route, 7)
            if route == w:
                z_copy(0, w, route, 8).start()
    for route in range(2):
        for way in range(2):
            by_copy(-7 if route == 0 else 7, 13 + route, way).start()
    for e in range(4):
        for route in range(2):
            z_wait(1, e, route, 7)
            if route == e // 2:
                z_copy(1, e, route, 8).start()
    y_stage(-6, 11)
    y_stage(6, 12)
    for w in range(2):
        z_wait(0, w, w, 8)
    for way in range(3):
        by_last(way).start()
    y_stage(-7, 13)
    y_stage(7, 14)
    for i in (4, 5):
        t_wait(i)
        d_copy(3, i - 4).start()
    for e in range(4):
        z_wait(1, e, e // 2, 8)

    got(tok.at[:, 0], td_r.at[0])
    for zh_ in range(2):
        u_local(zh_).wait()
        rcopy(ub.at[1 - c, zh_], ub.at[1 - c, zh_], u_s.at[zh_], u_r.at[zh_], twin).wait_recv()

    def third(g):
        def member(m, _):
            lo = tok[:, m, :, LOW : LOW + 128].reshape(4 * ROWS, 128)
            if g < 2:
                wi, wo = wb[g, 0].reshape(D, 256), wb[g, 1].reshape(D, 256)
                u = ub[m, g, :, 128:384]
            else:
                wi, wo = wa[0].reshape(D, 256), wa[1].reshape(D, 256)
                u = jnp.concatenate([ub[m, 0, :, 0:128], ub[m, 1, :, 0:128]], axis=1)
            pre = dot(tok[:, m, :, 0:D].reshape(4 * ROWS, D), wi) + dot(lo[:, 0:RANK], u)
            dhid = 0.5 * dot(tok[:, m, :, COT:WIDE].reshape(4 * ROWS, D), wo)
            sig = jax.nn.sigmoid(pre)
            dpre = (dhid * sig * (1.0 + pre * (1.0 - sig))).astype(BF16)
            part = dot(lo, dpre, ((0,), (0,)))
            for r in range(8):
                rss[g, m, r] = part[8 * r : 8 * r + 8].astype(BF16)
            for x_ in range(4):
                bp = dot(u, dpre[ROWS * x_ : ROWS * (x_ + 1)], ((1,), (1,)))
                if g == 2:
                    bks[x_, m] = bp
                else:
                    bks[x_, m] += bp
            return 0

        lax.fori_loop(0, 2, member, 0)

    def rs_copy(g, d, c_):
        return rcopy(
            rss.at[g, c_, (zl + d) % 8], rsr.at[g, zl, c], rs_s.at[g, c_], rs_r.at[g, c], zdev(d, c_)
        )

    def rs_other(g):
        return rcopy(rss.at[g, 1 - c, zl], rsr.at[g, zl, c], rs_s.at[g, 2], rs_r.at[g, 2], twin)

    def rs_start(g):
        for d in (4, 3, 5, 2, 6, 1, 7):
            for c_ in range(2):
                rs_copy(g, d, c_).start()
        rs_other(g).start()
        rsr[g, zl, c] = rss[g, c, zl]

    def rs_sum(g):
        got(rsr.at[g, zl, 1 - c], rs_r.at[g, 2])
        for c_ in range(2):
            got(rsr.at[g, 0:7, c_], rs_r.at[g, c_])
        for c_ in range(2):
            total = rsr[g, 0, c_].astype(F32)
            for i in range(1, 8):
                total = total + rsr[g, i, c_].astype(F32)
            agu[g, x, zl, :, 256 * c_ : 256 * (c_ + 1)] = total.astype(BF16)

    def bk_copy(d, c_):
        x_ = (x + d) % 4
        return rcopy(bks.at[x_, c_], bkr.at[x, c], bk_s.at[c_], bk_r.at[c], dev(x_, y, z, c_))

    def bk_other():
        return rcopy(bks.at[x, 1 - c], bkr.at[x, c], bk_s.at[2], bk_r.at[2], twin)

    def ba_copy(d):
        return rcopy(bka.at[x], bka.at[x], ba_s.at[0], ba_r.at[0], dev((x + d) % 4, y, z, c))

    def dn_copy(d):
        return rcopy(dns.at[(zl + d) % 8], dnr.at[zl], dn_s.at[0], dn_r.at[0], zdev(d, c))

    z4, q4 = (zl // 4) * 4, zl % 4
    far = (zl + 4) % 8

    def piece(g, zl_):
        return agd.at[x, zl_] if g == 3 else agu.at[g, x, zl_]

    def near(j):
        return dev(x, y, zh * 8 + z4 + (q4 + j) % 4, c)

    def gz_copy(g, j):
        if j == 0:
            return rcopy(piece(g, zl), piece(g, zl), gz_s.at[g], gz_r.at[g, 0], dev(x, y, zh * 8 + far, c))
        src = zl if j < 4 else far
        return rcopy(piece(g, src), piece(g, src), gz_s.at[g], gz_r.at[g, 1 if j < 4 else 2], near((j - 1) % 3 + 1))

    def gz_wait(g, i):
        got(agu.at[g, 0, 0:1] if i == 0 else agu.at[g, 0, 0:3], gz_r.at[g, i])

    def gz_all(g):
        for d in (4, 3, 5, 2, 6, 1, 7):
            rcopy(piece(g, zl), piece(g, zl), gz_s.at[g], gz_r.at[g, 0], zdev(d, c)).start()

    def gz_all_wait(g):
        got(agd.at[0, 0:7] if g == 3 else agu.at[g, 0, 0:7], gz_r.at[g, 0])

    def g_half(g, x_, h):
        return agu.at[g, x_, pl.ds(z4 if h == 0 else 4 - z4, 4)]

    def gx_copy(g, i):
        x_, h, to = [
            (x, 0, right), (x, 1, right), (x, 1, left), (x, 0, left), (xl, 0, right), (xr, 1, left)
        ][i]
        return rcopy(g_half(g, x_, h), g_half(g, x_, h), gx_s.at[g], gx_r.at[g, i], to)

    def gx_wait(g, i):
        x_, h = [(xl, 0), (xl, 1), (xr, 1), (xr, 0), (xo, 0), (xo, 1)][i]
        got(g_half(g, x_, h), gx_r.at[g, i])

    def gd_copy(d):
        return rcopy(agd.at[x], agd.at[x], gx_s.at[3], gx_r.at[3, 0], dev((x + d) % 4, y, z, c))

    def gz_own(g):
        for j in range(4):
            gz_copy(g, j).start()

    def gz_pass(g):
        gz_wait(g, 0)
        for j in range(4, 7):
            gz_copy(g, j).start()

    def gx_first(g):
        gz_wait(g, 1)
        gx_copy(g, 0).start()
        gx_copy(g, 3).start()

    def gx_second(g):
        gz_wait(g, 2)
        gx_copy(g, 2).start()
        gx_copy(g, 1).start()

    def gx_pass(g):
        gx_wait(g, 0)
        gx_copy(g, 4).start()
        gx_wait(g, 2)
        gx_copy(g, 5).start()

    third(2)
    rs_start(2)
    for way in range(3):
        by_last_wait(way)
    for way in range(2):
        got(wb.at[0, 0, 0:3, 0:5], bo_r.at[way])
    third(0)
    rs_start(0)
    third(1)
    for d in range(1, 4):
        for c_ in range(2):
            bk_copy(d, c_).start()
    bk_other().start()
    rs_start(1)
    bkr[x, c] = bks[x, c]

    got(bkr.at[x, 1 - c], bk_r.at[2])
    for c_ in range(2):
        got(bkr.at[0:3, c_], bk_r.at[c_])
    total = bkr[0, 0]
    for i in range(1, 8):
        total = total + bkr[i // 2, i % 2]
    bka[x] = total.astype(BF16)
    for d in range(1, 4):
        ba_copy(d).start()

    rs_sum(2)
    gz_own(2)
    rs_sum(0)
    gz_own(0)

    got(bka.at[0:3], ba_r.at[0])
    quarter = pl.ds(pl.multiple_of(x * 384, 128), 384)
    part = dot(bka[0], tok[0, c, :, quarter])
    for x_ in range(1, 4):
        part = part + dot(bka[x_], tok[x_, c, :, quarter])
    for r in range(8):
        dns[r] = part[8 * r : 8 * r + 8].astype(BF16)
    for d in range(1, 8):
        dn_copy(d).start()
    dnr[zl] = dns[zl]

    rs_sum(1)
    gz_own(1)
    gz_pass(2)
    gx_first(2)
    got(dnr.at[0:7], dn_r.at[0])
    total = dnr[0].astype(F32)
    for i in range(1, 8):
        total = total + dnr[i].astype(F32)
    agd[x, zl] = total.astype(BF16)
    gz_all(3)
    gz_pass(0)
    gx_first(0)
    gx_second(2)
    gz_pass(1)
    gx_second(0)
    gx_pass(2)
    gx_first(1)
    gx_second(1)
    gx_pass(0)
    gz_all_wait(3)
    for d in range(1, 4):
        gd_copy(d).start()
    gx_pass(1)
    outs = [pltpu.make_async_copy(agu.at[g], ou.at[g], o_s.at[g]) for g in range(3)]
    outs.append(pltpu.make_async_copy(agd, od, o_s.at[3]))
    for g in (2, 0, 1):
        for i in (1, 3, 4, 5):
            gx_wait(g, i)
        outs[g].start()
    got(agd.at[0:3], gx_r.at[3, 0])
    outs[3].start()

    @pl.when(x != y)
    def _():
        tb_copy().wait_send()
        ta_copy().wait_send()

    sent(wa.at[:, 0:3, 0, :, 0:128], ta_s.at[1])
    sent(tok.at[0:3, 0], tk_s.at[0])
    sent(tok.at[:, 0], td_s.at[0])
    for zh_ in range(2):
        u_copy(zh_).wait_send()
    for route in range(2):
        sent(wa.at[0:2, 0:3, 0:5], az_s.at[route])
        sent(wb.at[0, 0, 0:3, 0:5], bz_s.at[route])
        sent(wb.at[0, 0], by_s.at[route])
        sent(wb.at[0, 0, 0:3, 0:5], bo_s.at[route])
    sent(wb.at[0, 0, 0, 0:2], by_s.at[2])
    bk_other().wait_send()
    for c_ in range(2):
        sent(bks.at[0:3, 0], bk_s.at[c_])
    sent(bka.at[0:3], ba_s.at[0])
    sent(dns.at[0:7], dn_s.at[0])
    for g in range(3):
        rs_other(g).wait_send()
        for c_ in range(2):
            sent(rss.at[g, c_, 0:7], rs_s.at[g, c_])
        sent(agu.at[g, 0, 0:7], gz_s.at[g])
        sent(agu.at[g, 0:3], gx_s.at[g])
    sent(agd.at[0, 0:7], gz_s.at[3])
    sent(agd.at[0:3], gx_s.at[3])
    for out in outs:
        out.wait()


def spread(agu, agd, dn_out, up_out):
    def write(i, _):
        rows = pl.ds(pl.multiple_of(8 * i, 8), 8)
        for x_ in range(4):
            for c_ in range(2):
                lo = 256 * c_
                for h in range(2):
                    col = ((x_ * 2 + h) * 2 + c_) * 384
                    up_out[rows, col : col + 128] = agu[2, x_, i, :, lo + 128 * h : lo + 128 * (h + 1)].astype(F32)
                    up_out[rows, col + 128 : col + 384] = agu[h, x_, i, :, lo : lo + 256].astype(F32)
            dn_out[rows, 384 * x_ : 384 * (x_ + 1)] = agd[x_, i].astype(F32)
        return 0

    lax.fori_loop(0, 8, write, 0)


def on_device(frames, gain, w1, w2, down_map, up_map, lengths, cot):
    vmem = pl.BlockSpec(memory_space=pltpu.VMEM)
    hbm = pl.BlockSpec(memory_space=pl.ANY)
    dma = pltpu.SemaphoreType.DMA
    pieces = pl.pallas_call(
        kernel,
        out_shape=(
            jax.ShapeDtypeStruct((3, 4, 8, 8, 512), BF16),
            jax.ShapeDtypeStruct((4, 8, 8, 384), BF16),
        ),
        in_specs=[hbm, vmem, vmem, vmem, hbm, hbm, pl.BlockSpec(memory_space=pltpu.SMEM), hbm],
        out_specs=(pl.BlockSpec(memory_space=pl.ANY), pl.BlockSpec(memory_space=pl.ANY)),
        scratch_shapes=[
            pltpu.VMEM((3, 4, 8, 8, 512), BF16),
            pltpu.VMEM((4, 8, 8, 384), BF16),
            pltpu.VMEM((2, 48, 128), BF16),
            pltpu.VMEM((2, 48, 256), BF16),
            pltpu.VMEM((2, 4, 8, 48, 256), BF16),
            pltpu.VMEM((2, 2, 4, 8, 48, 256), BF16),
            pltpu.VMEM((4, 2, ROWS, WIDE), BF16),
            pltpu.VMEM((2, 2, RANK, 384), BF16),
            pltpu.VMEM((4, 2, RANK, ROWS), F32),
            pltpu.VMEM((4, 2, RANK, ROWS), F32),
            pltpu.VMEM((4, RANK, ROWS), BF16),
            pltpu.VMEM((3, 2, 8, 8, 256), BF16),
            pltpu.VMEM((3, 8, 2, 8, 256), BF16),
            pltpu.VMEM((8, 8, 384), BF16),
            pltpu.VMEM((8, 8, 384), BF16),
            dma((4,)), dma((4,)), dma((1,)), dma((1,)), dma((1,)), dma((6,)), dma((1,)), dma((1,)), dma((4,)), dma((2,)),
            dma((2,)), dma((2, 4, 8)), dma((2,)), dma((2, 2, 8)),
            dma((3,)), dma((3, 16)), dma((2,)), dma((2,)),
            dma((3,)), dma((3,)), dma((1,)), dma((1,)), dma((3, 3)), dma((3, 3)),
            dma((1,)), dma((1,)), dma((4,)), dma((4, 3)), dma((4,)), dma((4, 6)), dma((4,)),
            pltpu.VMEM((1, ROWS, D), BF16),
            pltpu.VMEM((1, ROWS, D), BF16),
            pltpu.VMEM((RANK, D), BF16),
            dma((3,)),
        ],
        compiler_params=pltpu.CompilerParams(
            collective_id=0, has_side_effects=True, vmem_limit_bytes=56 * 1024 * 1024
        ),
    )(frames, gain, w1, w2.T, down_map[0].T, up_map, lengths, cot)
    dn, up = pl.pallas_call(
        spread,
        out_shape=(
            jax.ShapeDtypeStruct((RANK, D), F32),
            jax.ShapeDtypeStruct((RANK, 6144), F32),
        ),
        in_specs=[vmem, vmem],
        out_specs=(vmem, vmem),
    )(*pieces)
    return dn.T[None], up[None]


def solution(mesh):
    in_specs = (
        P("member", "fsdp", None),
        P(),
        P("fsdp", "member"),
        P("member", "fsdp"),
        P("member", None, None),
        P("member", None, None),
        P("member", "fsdp"),
        P("member", "fsdp", None),
    )
    out_specs = (P("member", None, None), P("member", None, None))
    return jax.shard_map(
        on_device, mesh=mesh, in_specs=in_specs, out_specs=out_specs, check_vma=False
    )
```
